32 devices in a mesh: depth: 4 (over z), row: 8 (over y, x, core).
Axes of the slice: x: 2, y: 2, z: 4, core: 2. Of those that a mesh axis runs over, the one named last changes fastest.
Arguments:
- volume: float32 [192, 512, 2048], P('depth', 'row'), may hold values from -6 to 6
- transfer: float32 [8], replicated, may hold values from 0.3 to 1.2
Outputs:
- image: float32 [4, 512, 2048], P(None, 'row', 'depth')
The draws below stay inside these ranges and needn't reach their ends.
All inputs are finite; a program needn't handle non-finite values.
Results may differ from the reference program's by a relative error of at most 0.0003.
Values sent between devices are 32-bit elements; how exact they have to be, the bound alone decides.
No kernel may reach another device: no remote copies, remote signals or barrier semaphores. Data moves between devices by JAX's collectives and lax.ppermute only.
A program may use at most 192 MiB of HBM per device.

```python
import jax
import jax.numpy as jnp
from jax import lax

X = 2048
CY = 64
NZ = 192
NY = 512


def block_scale(rng, extent, cuts, least, high):
    gain, own = 1.0, jax.random.fold_in(rng, 6)
    for dim, blocks in cuts:
        draws = jnp.exp(jax.random.uniform(jax.random.fold_in(own, dim), (blocks,), jnp.float32, least / len(cuts), high / len(cuts)))
        gain = gain * jnp.repeat(draws, extent[dim] // blocks).reshape([-1 if axis == dim else 1 for axis in range(len(extent))])
    return gain


def bell_draw(key, shape, scale, bound, cuts=(), held_as=jnp.bfloat16):
    loudness = block_scale(key, shape, cuts, -0.22, 0.18) if cuts else 1.0
    drawn = jax.random.normal(key, shape, jnp.float32) * scale * loudness
    return jnp.minimum(jnp.maximum(drawn, -bound), bound).astype(held_as)


def setup_inputs(seed: int = 0) -> dict:
    keys = jax.random.split(jax.random.key(seed), 3)
    return {
        "volume": bell_draw(keys[0], (NZ, NY, X), 1.0, 6.0, ((0, 4), (1, 8)), jnp.float32),
        "transfer": jnp.clip(jax.random.uniform(keys[1], (8,), jnp.float32, 0.3, 1.2), 0.3, 1.2),
    }


def slope_cols(center):
    zero_col = jnp.zeros_like(center[..., :1])
    right = jnp.concatenate([center[..., 1:], zero_col], -1)
    left = jnp.concatenate([zero_col, center[..., :-1]], -1)
    return 0.5 * (right - left)

def emit(framed, transfer, slices):
    center = framed[1:-1, 1:-1, :]
    slope_depth = 0.5 * (framed[2:, 1:-1, :] - framed[:-2, 1:-1, :])
    slope_row = 0.5 * (framed[1:-1, 2:, :] - framed[1:-1, :-2, :])
    slope_col = slope_cols(center)
    inverse = lax.rsqrt(slope_depth * slope_depth + slope_row * slope_row + slope_col * slope_col + 1.0)
    lambert = jnp.abs((slope_depth + 2.0 * slope_row + 2.0 * slope_col) * inverse) / 3.0
    ambient = 0.5 * transfer[7]
    shading = ambient + (1.0 - ambient) * lambert
    depth_term = 2.0 * transfer[6] / slices * jax.nn.softplus(center)
    opacity = -jnp.expm1(-depth_term)
    tinting = jax.nn.sigmoid(2.0 * center)
    weight = shading * opacity
    emitted = jnp.stack([(transfer[channel] + transfer[3 + channel] * tinting) * weight for channel in range(3)])
    return (emitted, depth_term)

def reference(volume, transfer):
    blocks = NY // CY
    zero_slab = jnp.zeros((1, CY + 2, X), jnp.float32)

    def render(index):
        start = (index * CY).astype(jnp.int32)
        middle = lax.dynamic_slice_in_dim(volume, start, CY, 1)
        above = lax.dynamic_slice_in_dim(volume, jnp.maximum(start - 1, 0).astype(jnp.int32), 1, 1) * (index > 0).astype(jnp.float32)
        below = lax.dynamic_slice_in_dim(volume, jnp.minimum(start + CY, NY - 1).astype(jnp.int32), 1, 1) * (index < blocks - 1).astype(jnp.float32)
        framed = jnp.concatenate([above, middle, below], 1)
        framed = jnp.concatenate([zero_slab.astype(framed.dtype), framed, zero_slab.astype(framed.dtype)], 0)
        emitted, depth_term = emit(framed, transfer, NZ)
        before = jnp.cumsum(depth_term, 0) - depth_term
        color = lax.optimization_barrier(jnp.sum(jnp.exp(-before)[None] * emitted, 1))
        total = lax.optimization_barrier(jnp.sum(depth_term, 0))
        return jnp.concatenate([color, -jnp.expm1(-total)[None]], 0)
    pieces = lax.map(render, jnp.arange(blocks, dtype=jnp.int32))
    return jnp.transpose(pieces, (1, 0, 2, 3)).reshape(4, NY, X)
```

```python
import functools
import math

import jax
import jax.numpy as jnp
from jax import lax
from jax.experimental import pallas as pl
from jax.experimental.pallas import tpu as pltpu
from jax.sharding import PartitionSpec as P

LANES = 128
SUBLANES = 8
LN2 = math.log(2.0)


def halo(cells, axis, dim):
    count = lax.axis_size(axis)
    last = cells.shape[dim] - 1
    head = lax.slice_in_dim(cells, 0, 1, axis=dim)
    tail = lax.slice_in_dim(cells, last, last + 1, axis=dim)
    before = lax.ppermute(tail, axis, [(i, i + 1) for i in range(count - 1)])
    after = lax.ppermute(head, axis, [(i + 1, i) for i in range(count - 1)])
    return before, after


def cell(x, below, above, up, down, left, right, state, coef, ends):
    log_t, passing, shade, tinted = state
    gamma, ratio = coef
    first, last = ends
    to_right = pltpu.roll(jnp.where(first, right, x), LANES - 1, 1)
    to_left = pltpu.roll(jnp.where(last, left, x), 1, 1)
    d_col = to_right - to_left
    d_row = down - up
    d_depth = above - below
    plane = d_row + d_col
    along = d_depth + (plane + plane)
    norm = d_depth * d_depth + (d_row * d_row + (d_col * d_col + 4.0))
    lambert = jnp.abs(along) * lax.rsqrt(norm)
    log_t = log_t + gamma * jnp.log2(1.0 + jnp.exp(x))
    after = jnp.exp2(log_t)
    taken = passing - after
    lit = taken * lambert
    shade = shade + lit
    tinted = tinted + (taken + ratio * lit) * jnp.tanh(x)
    return log_t, after, shade, tinted


def spans(slices, parts):
    step = slices // parts
    edges = [0] + [step * (k + 1) + 1 for k in range(parts - 1)] + [slices]
    return [(edges[k], edges[k + 1] - edges[k]) for k in range(parts)]


def render_kernel(
    parts, tiles, block, coef, volume, before, after, above_row, below_row, out, cells, sems, edge_sems
):
    slices, rows, columns = volume.shape
    chunks = out.shape[2] // LANES
    total = columns // LANES
    base = block[0] * chunks
    step = slices // parts
    groups = rows // SUBLANES // tiles
    cuts = spans(slices, parts)
    has_left = base > 0
    has_right = base + chunks < total
    gamma, ratio = coef[0], coef[1]
    lane = lax.broadcasted_iota(jnp.int32, (SUBLANES, LANES), 1)
    ends = (lane == 0, lane == LANES - 1)
    zero = jnp.zeros((SUBLANES, LANES), jnp.float32)
    one = jnp.ones((SUBLANES, LANES), jnp.float32)

    def lanes_of(c):
        at = jnp.clip(base + (c - 1), 0, total - 1)
        return pl.ds(pl.multiple_of(at * LANES, LANES), LANES)

    def body_copy(c, k):
        start, size = cuts[k]
        return pltpu.make_async_copy(
            volume.at[pl.ds(start, size), :, lanes_of(c)],
            cells.at[c, pl.ds(start + 1, size), pl.ds(SUBLANES, rows), :],
            sems.at[c, k],
        )

    def edge_copies(c):
        at = lanes_of(c)
        inner = pl.ds(SUBLANES, rows)
        middle = pl.ds(1, slices)
        return [
            pltpu.make_async_copy(before.at[0, :, at], cells.at[c, 0, inner, :], edge_sems.at[c, 0]),
            pltpu.make_async_copy(
                after.at[0, :, at], cells.at[c, slices + 1, inner, :], edge_sems.at[c, 1]
            ),
            pltpu.make_async_copy(
                above_row.at[:, :, at],
                cells.at[c, middle, pl.ds(SUBLANES - 1, 1), :],
                edge_sems.at[c, 2],
            ),
            pltpu.make_async_copy(
                below_row.at[:, :, at],
                cells.at[c, middle, pl.ds(SUBLANES + rows, 1), :],
                edge_sems.at[c, 3],
            ),
        ]

    def clear(c):
        def slice_of(z, carry):
            for r in range(rows // SUBLANES):
                cells[c, z + 1, pl.ds(SUBLANES * (r + 1), SUBLANES), :] = zero
            return carry

        lax.fori_loop(0, slices, slice_of, 0)

    for copy in edge_copies(1):
        copy.start()
    for k in range(parts):
        body_copy(1, k).start()
        pl.when(has_left)(lambda k=k: body_copy(0, k).start())
        body_copy(2, k).start()
    for c in range(3, chunks + 1):
        for k in range(parts):
            body_copy(c, k).start()
    for k in range(parts):
        pl.when(has_right)(lambda k=k: body_copy(chunks + 1, k).start())
    for c in range(2, chunks + 1):
        for copy in edge_copies(c):
            copy.start()
    pl.when(jnp.logical_not(has_left))(lambda: clear(0))
    pl.when(jnp.logical_not(has_right))(lambda: clear(chunks + 1))

    def land(c, k):
        @pl.when(c == 1)
        def _():
            body_copy(1, k).wait()
            body_copy(2, k).wait()
            pl.when(has_left)(lambda: body_copy(0, k).wait())

        @pl.when(jnp.logical_and(c > 1, jnp.logical_or(c < chunks, has_right)))
        def _():
            body_copy(c + 1, k).wait()

    def group(index, carry):
        c = index // groups + 1
        row = pl.multiple_of((index % groups * tiles + 1) * SUBLANES, SUBLANES)
        fresh = index % groups == 0

        @pl.when(fresh)
        def _():
            land(c, 0)
            for copy in edge_copies(c):
                copy.wait()

        def march(k, carry):
            for part in range(1, parts):
                pl.when(jnp.logical_and(fresh, k == part))(lambda part=part: land(c, part))
            states, belows, centers = carry
            for i in range(step):
                z = k * step + (i + 1)
                marched, aboves = [], []
                for t in range(tiles):
                    at = row + SUBLANES * t
                    here = pl.ds(at, SUBLANES)
                    above = cells[c, z + 1, here, :]
                    marched.append(
                        cell(
                            centers[t],
                            belows[t],
                            above,
                            cells[c, z, pl.ds(at - 1, SUBLANES), :],
                            cells[c, z, pl.ds(at + 1, SUBLANES), :],
                            cells[c - 1, z, here, :],
                            cells[c + 1, z, here, :],
                            states[t],
                            (gamma, ratio),
                            ends,
                        )
                    )
                    aboves.append(above)
                states, belows, centers = marched, centers, aboves
            return states, belows, centers

        def rows_at(z):
            return [cells[c, z, pl.ds(row + SUBLANES * t, SUBLANES), :] for t in range(tiles)]

        carry = ([(zero, one, zero, zero)] * tiles, rows_at(0), rows_at(1))
        states, _, _ = lax.fori_loop(0, parts, march, carry)
        at_lanes = pl.ds(pl.multiple_of((c - 1) * LANES, LANES), LANES)
        for t in range(tiles):
            at_rows = pl.ds(pl.multiple_of(row + SUBLANES * (t - 1), SUBLANES), SUBLANES)
            log_t, _, shade, tinted = states[t]
            for channel, value in enumerate((shade, tinted, log_t)):
                out[channel, at_rows, at_lanes] = value
        return 0

    lax.fori_loop(0, chunks * groups, group, 0)


def render(block, coef, volume, edges, width, tiles=4, parts=4):
    slices, rows, _ = volume.shape
    chunks = width // LANES
    smem = pl.BlockSpec(memory_space=pltpu.SMEM)
    hbm = pl.BlockSpec(memory_space=pl.ANY)
    return pl.pallas_call(
        functools.partial(render_kernel, parts, tiles),
        in_specs=[smem, smem] + [hbm] * 5,
        out_specs=pl.BlockSpec(memory_space=pltpu.VMEM),
        out_shape=jax.ShapeDtypeStruct((3, rows, width), jnp.float32),
        scratch_shapes=[
            pltpu.VMEM((chunks + 2, slices + 2, rows + 2 * SUBLANES, LANES), jnp.float32),
            pltpu.SemaphoreType.DMA((chunks + 2, parts)),
            pltpu.SemaphoreType.DMA((chunks + 1, 4)),
        ],
        compiler_params=pltpu.CompilerParams(vmem_limit_bytes=32 << 20),
        name="render",
    )(block, coef, volume, *edges)


def on_device(volume, transfer):
    local_slices, local_rows, columns = volume.shape
    groups = lax.axis_size("depth")
    mine = lax.axis_index("depth")
    slices = local_slices * groups
    width = columns // groups
    edges = halo(volume, "depth", 0) + halo(volume, "row", 1)
    ambient = 0.5 * transfer[7]
    ratio = (1.0 - ambient) / (3.0 * ambient)
    coef = jnp.stack([-2.0 * transfer[6] / slices, ratio])
    shifts = sorted(range(1, groups), key=lambda s: -min(s, groups - s)) + [0]
    parts = []
    for shift in shifts:
        block = jnp.reshape((mine + shift) % groups, (1,)).astype(jnp.int32)
        part = render(block, coef, volume, edges, width)
        if shift:
            pairs = [(i, (i + shift) % groups) for i in range(groups)]
            part = lax.ppermute(part, "depth", pairs)
        parts.append(part)
    sources = [(mine - shift) % groups for shift in shifts]
    shade = tinted = log_t = 0.0
    for i, part in enumerate(parts):
        ahead = 0.0
        for j, other in enumerate(parts):
            if i != j:
                ahead = ahead + jnp.where(sources[j] < sources[i], other[2], 0.0)
        passing = jnp.exp2(ahead)
        shade = shade + passing * part[0]
        tinted = tinted + passing * part[1]
        log_t = log_t + part[2]
    opacity = -jnp.expm1(LN2 * log_t)
    full = ambient * (opacity + ratio * shade)
    tinted = ambient * tinted
    base = [transfer[c] * full + transfer[3 + c] * (0.5 * (full + tinted)) for c in range(3)]
    return jnp.stack(base + [opacity])


def solution(mesh):
    in_specs = (P("depth", "row", None), P())
    out_specs = P(None, "row", "depth")
    return jax.shard_map(
        on_device, mesh=mesh, in_specs=in_specs, out_specs=out_specs, check_vma=False
    )
```

```python
import functools
import math

import jax
import jax.numpy as jnp
from jax import lax
from jax.experimental import pallas as pl
from jax.experimental.pallas import tpu as pltpu
from jax.sharding import PartitionSpec as P

LANES = 128
SUBLANES = 8
LN2 = math.log(2.0)
SMEM = pl.BlockSpec(memory_space=pltpu.SMEM)
VMEM = pl.BlockSpec(memory_space=pltpu.VMEM)
ANY = pl.BlockSpec(memory_space=pl.ANY)


def cut_kernel(volume, first, last, top, bottom, sems):
    slices, rows, _ = volume.shape
    copies = [
        pltpu.make_async_copy(source, target, sems.at[i])
        for i, (source, target) in enumerate(
            [
                (volume.at[pl.ds(0, 1)], first),
                (volume.at[pl.ds(slices - 1, 1)], last),
                (volume.at[:, pl.ds(0, 1), :], top),
                (volume.at[:, pl.ds(rows - 1, 1), :], bottom),
            ]
        )
    ]
    for copy in copies:
        copy.start()
    for copy in copies:
        copy.wait()


def cut(volume):
    slices, rows, columns = volume.shape
    slab = jax.ShapeDtypeStruct((1, rows, columns), jnp.float32)
    strip = jax.ShapeDtypeStruct((slices, 1, columns), jnp.float32)
    return pl.pallas_call(
        cut_kernel,
        in_specs=[ANY],
        out_specs=[ANY] * 4,
        out_shape=[slab, slab, strip, strip],
        scratch_shapes=[pltpu.SemaphoreType.DMA((4,))],
        name="cut",
    )(volume)


def pass_on(value, axis, forward):
    count = lax.axis_size(axis)
    pairs = [(i, i + 1) if forward else (i + 1, i) for i in range(count - 1)]
    return lax.ppermute(value, axis, pairs)


def tile_constants():
    lane = lax.broadcasted_iota(jnp.int32, (SUBLANES, LANES), 1)
    return lane == 0, lane == LANES - 1


def coefficients(transfer, slices):
    gamma = jnp.full((SUBLANES, LANES), transfer[6], jnp.float32) * (-2.0 / slices)
    ambient = 0.5 * jnp.full((SUBLANES, LANES), transfer[7], jnp.float32)
    return gamma, (1.0 - ambient) / (3.0 * ambient)


def cell(cells, c, z, row, x, below, above, state, coef, ends):
    log_t, passing, shade, tinted = state
    gamma, ratio = coef
    first, last = ends
    here = pl.ds(row, SUBLANES)
    right = cells[c + 1, z, here, :]
    left = cells[c - 1, z, here, :]
    d_row = cells[c, z, pl.ds(row + 1, SUBLANES), :] - cells[c, z, pl.ds(row - 1, SUBLANES), :]
    to_right = pltpu.roll(jnp.where(first, right, x), LANES - 1, 1)
    to_left = pltpu.roll(jnp.where(last, left, x), 1, 1)
    d_col = to_right - to_left
    d_depth = above - below
    plane = d_row + d_col
    along = d_depth + (plane + plane)
    norm = d_depth * d_depth + (d_row * d_row + (d_col * d_col + 4.0))
    lambert = jnp.abs(along) * lax.rsqrt(norm)
    log_t = log_t + gamma * jnp.log2(1.0 + jnp.exp(x))
    after = jnp.exp2(log_t)
    taken = passing - after
    lit = taken * lambert
    shade = shade + lit
    tinted = tinted + (taken + ratio * lit) * jnp.tanh(x)
    return log_t, after, shade, tinted


def fresh_state():
    zero = jnp.zeros((SUBLANES, LANES), jnp.float32)
    return zero, jnp.ones((SUBLANES, LANES), jnp.float32), zero, zero


def put(out, c, row, state):
    log_t, _, shade, tinted = state
    rows = pl.ds(row - SUBLANES, SUBLANES)
    lanes = pl.ds((c - 1) * LANES, LANES)
    if not isinstance(row, int):
        rows = pl.ds(pl.multiple_of(row - SUBLANES, SUBLANES), SUBLANES)
    if not isinstance(c, int):
        lanes = pl.ds(pl.multiple_of((c - 1) * LANES, LANES), LANES)
    for channel, value in enumerate((shade, tinted, log_t)):
        out[channel, rows, lanes] = value


class Bricks:
    def __init__(self, volume, cells, sems, shift, chunks, pieces):
        self.volume, self.cells, self.sems, self.pieces = volume, cells, sems, pieces
        self.chunks = chunks
        self.total = volume.shape[2] // LANES
        block = lax.rem(lax.axis_index("depth") + shift, lax.axis_size("depth"))
        self.base = block * chunks
        self.has_left = self.base > 0
        self.has_right = self.base + chunks < self.total

    def lanes(self, c):
        at = jnp.clip(self.base + (c - 1), 0, self.total - 1)
        return pl.ds(pl.multiple_of(at * LANES, LANES), LANES)

    def copy(self, c, k):
        z, depth, y, height = self.pieces[k]
        return pltpu.make_async_copy(
            self.volume.at[pl.ds(z, depth), pl.ds(y, height), self.lanes(c)],
            self.cells.at[c, pl.ds(z + 1, depth), pl.ds(y + SUBLANES, height), :],
            self.sems.at[c, k],
        )

    def clear(self, c):
        slices, rows, _ = self.volume.shape
        zero = jnp.zeros((SUBLANES, LANES), jnp.float32)

        def slice_of(z, carry):
            for r in range(rows // SUBLANES):
                self.cells[c, z + 1, pl.ds(SUBLANES * (r + 1), SUBLANES), :] = zero
            return carry

        lax.fori_loop(0, slices, slice_of, 0)

    def start(self, k, chunks):
        for c in chunks:
            if c == 0:
                pl.when(self.has_left)(lambda: self.copy(0, k).start())
            elif c == self.chunks + 1:
                pl.when(self.has_right)(lambda: self.copy(self.chunks + 1, k).start())
            else:
                self.copy(c, k).start()

    def start_all(self):
        for k in range(len(self.pieces)):
            self.start(k, (1, 0, 2))
        for c in range(3, self.chunks + 2):
            for k in range(len(self.pieces)):
                self.start(k, (c,))
        pl.when(jnp.logical_not(self.has_left))(lambda: self.clear(0))
        pl.when(jnp.logical_not(self.has_right))(lambda: self.clear(self.chunks + 1))

    def land(self, c, k):
        @pl.when(c == 1)
        def _():
            self.copy(1, k).wait()
            self.copy(2, k).wait()
            pl.when(self.has_left)(lambda: self.copy(0, k).wait())

        @pl.when(jnp.logical_and(c > 1, jnp.logical_or(c < self.chunks, self.has_right)))
        def _():
            self.copy(c + 1, k).wait()


def edge_copies(bricks, edges, sems, c):
    before, after, above_row, below_row = edges
    slices, rows, _ = bricks.volume.shape
    cells, at = bricks.cells, bricks.lanes(c)
    inner = pl.ds(SUBLANES, rows)
    middle = pl.ds(1, slices)
    pairs = [
        (before.at[0, :, at], cells.at[c, 0, inner, :]),
        (after.at[0, :, at], cells.at[c, slices + 1, inner, :]),
        (above_row.at[:, :, at], cells.at[c, middle, pl.ds(SUBLANES - 1, 1), :]),
        (below_row.at[:, :, at], cells.at[c, middle, pl.ds(SUBLANES + rows, 1), :]),
    ]
    return [pltpu.make_async_copy(*pair, sems.at[c, i]) for i, pair in enumerate(pairs)]


def march(cells, c, rows, begin, step, trips, coef, ends, arrive):
    def at(z):
        return [cells[c, z, pl.ds(row, SUBLANES), :] for row in rows]

    def trip(k, carry):
        arrive(k)
        states, belows, centers = carry
        for i in range(step):
            z = begin + 1 + k * step + i
            aboves = at(z + 1)
            states = [
                cell(cells, c, z, *tile, coef, ends)
                for tile in zip(rows, centers, belows, aboves, states)
            ]
            belows, centers = centers, aboves
        return states, belows, centers

    carry = ([fresh_state()] * len(rows), at(begin), at(begin + 1))
    if trips == 1:
        return trip(0, carry)[0]
    return lax.fori_loop(0, trips, trip, carry)[0]


def full_kernel(shift, tiles, pieces, total_slices, transfer, volume, *refs):
    *edges, out, cells, sems, edge_sems = refs
    slices, rows, _ = volume.shape
    chunks = out.shape[2] // LANES
    trips = len(pieces)
    groups = rows // SUBLANES // tiles
    bricks = Bricks(volume, cells, sems, shift, chunks, pieces)
    for copy in edge_copies(bricks, edges, edge_sems, 1):
        copy.start()
    bricks.start_all()
    for c in range(2, chunks + 1):
        for copy in edge_copies(bricks, edges, edge_sems, c):
            copy.start()
    coef = coefficients(transfer, total_slices)
    ends = tile_constants()

    def group(index, carry):
        c = index // groups + 1
        row = pl.multiple_of((index % groups * tiles + 1) * SUBLANES, SUBLANES)
        fresh = index % groups == 0

        @pl.when(fresh)
        def _():
            for copy in edge_copies(bricks, edges, edge_sems, c):
                copy.wait()
            bricks.land(c, 0)

        def arrive(k):
            for part in range(1, trips):
                pl.when(jnp.logical_and(fresh, k == part))(lambda part=part: bricks.land(c, part))

        at_rows = [row + SUBLANES * t for t in range(tiles)]
        states = march(cells, c, at_rows, 0, slices // trips, trips, coef, ends, arrive)
        for at_row, state in zip(at_rows, states):
            put(out, c, at_row, state)
        return carry

    lax.fori_loop(0, chunks * groups, group, 0)


def inner_kernel(shift, pieces, total_slices, transfer, volume, out, cells, sems):
    slices, rows, _ = volume.shape
    chunks = out.shape[2] // LANES
    trips = len(pieces)
    bricks = Bricks(volume, cells, sems, shift, chunks, pieces)
    bricks.start_all()
    coef = coefficients(transfer, total_slices)
    ends = tile_constants()
    at_rows = [SUBLANES * (t + 2) for t in range(rows // SUBLANES - 2)]

    def group(index, carry):
        c = index + 1
        bricks.land(c, 0)

        def arrive(k):
            for part in range(1, trips):
                pl.when(k == part)(lambda part=part: bricks.land(c, part))

        states = march(
            cells, c, at_rows, 1, (slices - 2) // trips, trips, coef, ends, arrive
        )
        for at_row, state in zip(at_rows, states):
            put(out, c, at_row, state)
        return carry

    lax.fori_loop(0, chunks, group, 0)


def rest_kernel(shift, pieces, total_slices, transfer, volume, *refs):
    *edges, inner, out, cells, sems, edge_sems = refs
    slices, rows, _ = volume.shape
    chunks = out.shape[2] // LANES
    bricks = Bricks(volume, cells, sems, shift, chunks, pieces)
    for copy in edge_copies(bricks, edges, edge_sems, 1):
        copy.start()
    bricks.start_all()
    for c in range(2, chunks + 1):
        for copy in edge_copies(bricks, edges, edge_sems, c):
            copy.start()
    coef = coefficients(transfer, total_slices)
    ends = tile_constants()

    def group(index, carry):
        c = index + 1
        for copy in edge_copies(bricks, edges, edge_sems, c):
            copy.wait()
        for k in range(len(pieces)):
            bricks.land(c, k)
        outer = [SUBLANES, rows]
        states = march(cells, c, outer, 0, slices, 1, coef, ends, lambda k: None)
        for at_row, state in zip(outer, states):
            put(out, c, at_row, state)
        lanes = pl.ds(pl.multiple_of((c - 1) * LANES, LANES), LANES)
        for t in range(1, rows // SUBLANES - 1):
            row = SUBLANES * (t + 1)
            here = pl.ds(row, SUBLANES)
            sides = []
            for z in (1, slices):
                below, x, above = [cells[c, z + i, here, :] for i in (-1, 0, 1)]
                sides.append(cell(cells, c, z, row, x, below, above, fresh_state(), coef, ends))
            (log_a, pass_a, shade_a, tint_a), (log_b, _, shade_b, tint_b) = sides
            shade, tint, log_t = [inner[i, pl.ds(row - SUBLANES, SUBLANES), lanes] for i in range(3)]
            passing = jnp.exp2(log_t)
            shade = shade_a + pass_a * (shade + passing * shade_b)
            tint = tint_a + pass_a * (tint + passing * tint_b)
            put(out, c, row, (log_a + log_t + log_b, None, shade, tint))
        return carry

    lax.fori_loop(0, chunks, group, 0)


def render(kernel, pieces, name, transfer, volume, extra, width, halo):
    slices, rows, columns = volume.shape
    chunks = width // LANES
    scratch = [
        pltpu.VMEM((chunks + 2, slices + 2, rows + 2 * SUBLANES, LANES), jnp.float32),
        pltpu.SemaphoreType.DMA((chunks + 2, len(pieces))),
    ]
    if halo:
        scratch.append(pltpu.SemaphoreType.DMA((chunks + 1, 4)))
    return pl.pallas_call(
        kernel,
        in_specs=[SMEM, ANY] + [ANY] * min(4, len(extra)) + [VMEM] * (len(extra) - 4),
        out_specs=VMEM,
        out_shape=jax.ShapeDtypeStruct((3, rows, width), jnp.float32),
        scratch_shapes=scratch,
        compiler_params=pltpu.CompilerParams(vmem_limit_bytes=32 << 20),
        name=name,
    )(transfer, volume, *extra)


def merge_kernel(shifts, transfer, *refs):
    *parts, out = refs
    count = len(parts)
    mine = lax.axis_index("depth")
    rows, width = out.shape[1:]
    sources = [lax.rem(mine - shift + count, count) for shift in shifts]
    nearer = [
        [jnp.where(sources[j] < sources[i], 1.0, 0.0) for j in range(count)] for i in range(count)
    ]
    ambient = 0.5 * jnp.full((SUBLANES, LANES), transfer[7], jnp.float32)
    spread = (1.0 - ambient) / 3.0

    def band(r, carry):
        here = pl.ds(pl.multiple_of(r * SUBLANES, SUBLANES), SUBLANES)
        for x in range(width // LANES):
            at = pl.ds(x * LANES, LANES)
            shade = tinted = log_t = jnp.zeros((SUBLANES, LANES), jnp.float32)
            logs = [part[2, here, at] for part in parts]
            for i, part in enumerate(parts):
                ahead = sum(logs[j] * nearer[i][j] for j in range(count) if j != i)
                passing = jnp.exp2(ahead)
                shade = shade + passing * part[0, here, at]
                tinted = tinted + passing * part[1, here, at]
                log_t = log_t + logs[i]
            half = jnp.tanh(log_t * (-0.5 * LN2))
            opacity = (half + half) / (1.0 + half)
            full = ambient * opacity + spread * shade
            mixed = 0.5 * (full + ambient * tinted)
            for color in range(3):
                out[color, here, at] = transfer[color] * full + transfer[3 + color] * mixed
            out[3, here, at] = opacity
        return carry

    lax.fori_loop(0, rows // SUBLANES, band, 0)


def merge(parts, shifts, transfer):
    _, rows, width = parts[0].shape
    return pl.pallas_call(
        functools.partial(merge_kernel, shifts),
        in_specs=[SMEM] + [VMEM] * len(parts),
        out_specs=VMEM,
        out_shape=jax.ShapeDtypeStruct((4, rows, width), jnp.float32),
        compiler_params=pltpu.CompilerParams(vmem_limit_bytes=16 << 20),
        name="merge",
    )(transfer, *parts)


def on_device(volume, transfer):
    slices, rows, columns = volume.shape
    groups = lax.axis_size("depth")
    total_slices = slices * groups
    width = columns // groups
    first, last, top, bottom = cut(volume)
    edges = (
        pass_on(last, "depth", True),
        pass_on(first, "depth", False),
        pass_on(bottom, "row", True),
        pass_on(top, "row", False),
    )
    half = slices // 2
    halves = [(0, half + 1, 0, rows), (half + 1, slices - half - 1, 0, rows)]
    ring = [
        (0, slices, 0, 2 * SUBLANES),
        (0, slices, rows - 2 * SUBLANES, 2 * SUBLANES),
        (0, 2, 2 * SUBLANES, rows - 4 * SUBLANES),
        (slices - 2, 2, 2 * SUBLANES, rows - 4 * SUBLANES),
    ]
    shifts = sorted(range(1, groups), key=lambda s: -min(s, groups - s)) + [0]
    parts = []
    for shift in shifts:
        if not parts:
            kernel = functools.partial(inner_kernel, shift, halves, total_slices)
            inner = render(kernel, halves, "inner", transfer, volume, (), width, False)
            kernel = functools.partial(rest_kernel, shift, ring, total_slices)
            part = render(kernel, ring, "rest", transfer, volume, edges + (inner,), width, True)
        else:
            kernel = functools.partial(full_kernel, shift, 8, halves, total_slices)
            part = render(kernel, halves, "full", transfer, volume, edges, width, True)
        if shift:
            pairs = [(i, (i + shift) % groups) for i in range(groups)]
            part = lax.ppermute(part, "depth", pairs)
        parts.append(part)
    return merge(parts, shifts, transfer)


def solution(mesh):
    in_specs = (P("depth", "row", None), P())
    out_specs = P(None, "row", "depth")
    return jax.shard_map(
        on_device, mesh=mesh, in_specs=in_specs, out_specs=out_specs, check_vma=False
    )
```

```python
import functools
import math

import jax
import jax.numpy as jnp
from jax import lax
from jax.experimental import pallas as pl
from jax.experimental.pallas import tpu as pltpu
from jax.sharding import PartitionSpec as P


LANES = 128
SUBLANES = 8
LN2 = math.log(2.0)
SMEM = pl.BlockSpec(memory_space=pltpu.SMEM)
VMEM = pl.BlockSpec(memory_space=pltpu.VMEM)
ANY = pl.BlockSpec(memory_space=pl.ANY)


def cut_kernel(volume, first, last, top, bottom, sems):
    slices, rows, _ = volume.shape
    copies = [
        pltpu.make_async_copy(source, target, sems.at[i])
        for i, (source, target) in enumerate(
            [
                (volume.at[pl.ds(0, 1)], first),
                (volume.at[pl.ds(slices - 1, 1)], last),
                (volume.at[:, pl.ds(0, 1), :], top),
                (volume.at[:, pl.ds(rows - 1, 1), :], bottom),
            ]
        )
    ]
    for copy in copies:
        copy.start()
    for copy in copies:
        copy.wait()


def cut(volume):
    slices, rows, columns = volume.shape
    slab = jax.ShapeDtypeStruct((1, rows, columns), jnp.float32)
    strip = jax.ShapeDtypeStruct((slices, 1, columns), jnp.float32)
    return pl.pallas_call(
        cut_kernel,
        in_specs=[ANY],
        out_specs=[VMEM] * 4,
        out_shape=[slab, slab, strip, strip],
        scratch_shapes=[pltpu.SemaphoreType.DMA((4,))],
        name="cut",
    )(volume)


def pass_on(value, axis, forward):
    count = lax.axis_size(axis)
    pairs = [(i, i + 1) if forward else (i + 1, i) for i in range(count - 1)]
    return lax.ppermute(value, axis, pairs)


def tile_constants():
    lane = lax.broadcasted_iota(jnp.int32, (SUBLANES, LANES), 1)
    return lane == 0, lane == LANES - 1


def coefficients(transfer, slices):
    gamma = jnp.full((SUBLANES, LANES), transfer[6], jnp.float32) * (-2.0 / slices)
    ambient = 0.5 * jnp.full((SUBLANES, LANES), transfer[7], jnp.float32)
    return gamma, (1.0 - ambient) / (3.0 * ambient)


def cell(cells, c, z, row, x, below, above, state, coef, ends):
    log_t, passing, shade, tinted = state
    gamma, ratio = coef
    first, last = ends
    here = pl.ds(row, SUBLANES)
    right = cells[c + 1, z, here, :]
    left = cells[c - 1, z, here, :]
    d_row = cells[c, z, pl.ds(row + 1, SUBLANES), :] - cells[c, z, pl.ds(row - 1, SUBLANES), :]
    to_right = pltpu.roll(jnp.where(first, right, x), LANES - 1, 1)
    to_left = pltpu.roll(jnp.where(last, left, x), 1, 1)
    d_col = to_right - to_left
    d_depth = above - below
    plane = d_row + d_col
    along = d_depth + (plane + plane)
    norm = d_depth * d_depth + (d_row * d_row + (d_col * d_col + 4.0))
    lambert = jnp.abs(along) * lax.rsqrt(norm)
    log_t = log_t + gamma * jnp.log2(1.0 + jnp.exp(x))
    after = jnp.exp2(log_t)
    taken = passing - after
    lit = taken * lambert
    shade = shade + lit
    tinted = tinted + (taken + ratio * lit) * jnp.tanh(x)
    return log_t, after, shade, tinted


def fresh_state():
    zero = jnp.zeros((SUBLANES, LANES), jnp.float32)
    return zero, jnp.ones((SUBLANES, LANES), jnp.float32), zero, zero


def put(out, c, row, state):
    log_t, _, shade, tinted = state
    rows = pl.ds(row - SUBLANES, SUBLANES)
    lanes = pl.ds((c - 1) * LANES, LANES)
    if not isinstance(row, int):
        rows = pl.ds(pl.multiple_of(row - SUBLANES, SUBLANES), SUBLANES)
    if not isinstance(c, int):
        lanes = pl.ds(pl.multiple_of((c - 1) * LANES, LANES), LANES)
    for channel, value in enumerate((shade, tinted, log_t)):
        out[channel, rows, lanes] = value


class Bricks:
    def __init__(self, volume, cells, sems, shift, chunks, pieces):
        self.volume, self.cells, self.sems, self.pieces = volume, cells, sems, pieces
        self.chunks = chunks
        self.total = volume.shape[2] // LANES
        block = lax.rem(lax.axis_index("depth") + shift, lax.axis_size("depth"))
        self.base = block * chunks
        self.has_left = self.base > 0
        self.has_right = self.base + chunks < self.total

    def lanes(self, c):
        at = jnp.clip(self.base + (c - 1), 0, self.total - 1)
        return pl.ds(pl.multiple_of(at * LANES, LANES), LANES)

    def copy(self, c, k):
        z, depth, y, height = self.pieces[k]
        return pltpu.make_async_copy(
            self.volume.at[pl.ds(z, depth), pl.ds(y, height), self.lanes(c)],
            self.cells.at[c, pl.ds(z + 1, depth), pl.ds(y + SUBLANES, height), :],
            self.sems.at[c, k],
        )

    def clear(self, c):
        slices, rows, _ = self.volume.shape
        zero = jnp.zeros((SUBLANES, LANES), jnp.float32)

        def slice_of(z, carry):
            for r in range(rows // SUBLANES):
                self.cells[c, z + 1, pl.ds(SUBLANES * (r + 1), SUBLANES), :] = zero
            return carry

        lax.fori_loop(0, slices, slice_of, 0)

    def start(self, k, chunks):
        for c in chunks:
            if c == 0:
                pl.when(self.has_left)(lambda: self.copy(0, k).start())
            elif c == self.chunks + 1:
                pl.when(self.has_right)(lambda: self.copy(self.chunks + 1, k).start())
            else:
                self.copy(c, k).start()

    def start_all(self):
        for k in range(len(self.pieces)):
            self.start(k, (1, 0, 2))
        for c in range(3, self.chunks + 2):
            for k in range(len(self.pieces)):
                self.start(k, (c,))
        pl.when(jnp.logical_not(self.has_left))(lambda: self.clear(0))
        pl.when(jnp.logical_not(self.has_right))(lambda: self.clear(self.chunks + 1))

    def land(self, c, k):
        @pl.when(c == 1)
        def _():
            self.copy(1, k).wait()
            self.copy(2, k).wait()
            pl.when(self.has_left)(lambda: self.copy(0, k).wait())

        @pl.when(jnp.logical_and(c > 1, jnp.logical_or(c < self.chunks, self.has_right)))
        def _():
            self.copy(c + 1, k).wait()


def edge_copies(bricks, edges, sems, c):
    before, after, above_row, below_row = edges
    slices, rows, _ = bricks.volume.shape
    cells, at = bricks.cells, bricks.lanes(c)
    inner = pl.ds(SUBLANES, rows)
    middle = pl.ds(1, slices)
    pairs = [
        (before.at[0, :, at], cells.at[c, 0, inner, :]),
        (after.at[0, :, at], cells.at[c, slices + 1, inner, :]),
        (above_row.at[:, :, at], cells.at[c, middle, pl.ds(SUBLANES - 1, 1), :]),
        (below_row.at[:, :, at], cells.at[c, middle, pl.ds(SUBLANES + rows, 1), :]),
    ]
    return [pltpu.make_async_copy(*pair, sems.at[c, i]) for i, pair in enumerate(pairs)]


def march(cells, c, rows, begin, step, trips, coef, ends, arrive):
    def at(z):
        return [cells[c, z, pl.ds(row, SUBLANES), :] for row in rows]

    def trip(k, carry):
        arrive(k)
        states, belows, centers = carry
        for i in range(step):
            z = begin + 1 + k * step + i
            aboves = at(z + 1)
            states = [
                cell(cells, c, z, *tile, coef, ends)
                for tile in zip(rows, centers, belows, aboves, states)
            ]
            belows, centers = centers, aboves
        return states, belows, centers

    carry = ([fresh_state()] * len(rows), at(begin), at(begin + 1))
    if trips == 1:
        return trip(0, carry)[0]
    return lax.fori_loop(0, trips, trip, carry)[0]


def full_kernel(shift, tiles, pieces, total_slices, transfer, volume, *refs):
    *edges, out, cells, sems, edge_sems = refs
    slices, rows, _ = volume.shape
    chunks = out.shape[2] // LANES
    trips = len(pieces)
    groups = rows // SUBLANES // tiles
    bricks = Bricks(volume, cells, sems, shift, chunks, pieces)
    for copy in edge_copies(bricks, edges, edge_sems, 1):
        copy.start()
    bricks.start_all()
    for c in range(2, chunks + 1):
        for copy in edge_copies(bricks, edges, edge_sems, c):
            copy.start()
    coef = coefficients(transfer, total_slices)
    ends = tile_constants()

    def group(index, carry):
        c = index // groups + 1
        row = pl.multiple_of((index % groups * tiles + 1) * SUBLANES, SUBLANES)
        fresh = index % groups == 0

        @pl.when(fresh)
        def _():
            for copy in edge_copies(bricks, edges, edge_sems, c):
                copy.wait()
            bricks.land(c, 0)

        def arrive(k):
            for part in range(1, trips):
                pl.when(jnp.logical_and(fresh, k == part))(lambda part=part: bricks.land(c, part))

        at_rows = [row + SUBLANES * t for t in range(tiles)]
        states = march(cells, c, at_rows, 0, slices // trips, trips, coef, ends, arrive)
        for at_row, state in zip(at_rows, states):
            put(out, c, at_row, state)
        return carry

    lax.fori_loop(0, chunks * groups, group, 0)


def inner_kernel(shift, pieces, total_slices, transfer, volume, out, cells, sems):
    slices, rows, _ = volume.shape
    chunks = out.shape[2] // LANES
    trips = len(pieces)
    bricks = Bricks(volume, cells, sems, shift, chunks, pieces)
    bricks.start_all()
    coef = coefficients(transfer, total_slices)
    ends = tile_constants()
    at_rows = [SUBLANES * (t + 2) for t in range(rows // SUBLANES - 2)]

    def group(index, carry):
        c = index + 1
        bricks.land(c, 0)

        def arrive(k):
            for part in range(1, trips):
                pl.when(k == part)(lambda part=part: bricks.land(c, part))

        states = march(
            cells, c, at_rows, 1, (slices - 2) // trips, trips, coef, ends, arrive
        )
        for at_row, state in zip(at_rows, states):
            put(out, c, at_row, state)
        return carry

    lax.fori_loop(0, chunks, group, 0)


def rest_kernel(shift, pieces, total_slices, transfer, volume, *refs):
    *edges, inner, out, cells, sems, edge_sems = refs
    slices, rows, _ = volume.shape
    chunks = out.shape[2] // LANES
    bricks = Bricks(volume, cells, sems, shift, chunks, pieces)
    for copy in edge_copies(bricks, edges, edge_sems, 1):
        copy.start()
    bricks.start_all()
    for c in range(2, chunks + 1):
        for copy in edge_copies(bricks, edges, edge_sems, c):
            copy.start()
    coef = coefficients(transfer, total_slices)
    ends = tile_constants()

    def group(index, carry):
        c = index + 1
        for copy in edge_copies(bricks, edges, edge_sems, c):
            copy.wait()
        for k in range(len(pieces)):
            bricks.land(c, k)
        outer = [SUBLANES, rows]
        states = march(cells, c, outer, 0, slices, 1, coef, ends, lambda k: None)
        for at_row, state in zip(outer, states):
            put(out, c, at_row, state)
        lanes = pl.ds(pl.multiple_of((c - 1) * LANES, LANES), LANES)
        for t in range(1, rows // SUBLANES - 1):
            row = SUBLANES * (t + 1)
            here = pl.ds(row, SUBLANES)
            sides = []
            for z in (1, slices):
                below, x, above = [cells[c, z + i, here, :] for i in (-1, 0, 1)]
                sides.append(cell(cells, c, z, row, x, below, above, fresh_state(), coef, ends))
            (log_a, pass_a, shade_a, tint_a), (log_b, _, shade_b, tint_b) = sides
            shade, tint, log_t = [inner[i, pl.ds(row - SUBLANES, SUBLANES), lanes] for i in range(3)]
            passing = jnp.exp2(log_t)
            shade = shade_a + pass_a * (shade + passing * shade_b)
            tint = tint_a + pass_a * (tint + passing * tint_b)
            put(out, c, row, (log_a + log_t + log_b, None, shade, tint))
        return carry

    lax.fori_loop(0, chunks, group, 0)


def render(kernel, pieces, transfer, volume, extra, width, halo):
    slices, rows, _ = volume.shape
    chunks = width // LANES
    scratch = [
        pltpu.VMEM((chunks + 2, slices + 2, rows + 2 * SUBLANES, LANES), jnp.float32),
        pltpu.SemaphoreType.DMA((chunks + 2, len(pieces))),
    ]
    if halo:
        scratch.append(pltpu.SemaphoreType.DMA((chunks + 1, 4)))
    return pl.pallas_call(
        kernel,
        in_specs=[SMEM, ANY] + [ANY] * min(4, len(extra)) + [VMEM] * (len(extra) - 4),
        out_specs=VMEM,
        out_shape=jax.ShapeDtypeStruct((3, rows, width), jnp.float32),
        scratch_shapes=scratch,
        compiler_params=pltpu.CompilerParams(vmem_limit_bytes=32 << 20),
    )(transfer, volume, *extra)


def merge_kernel(shifts, transfer, *refs):
    *parts, out = refs
    count = len(parts)
    mine = lax.axis_index("depth")
    rows, width = out.shape[1:]
    sources = [lax.rem(mine - shift + count, count) for shift in shifts]
    nearer = [
        [jnp.where(sources[j] < sources[i], 1.0, 0.0) for j in range(count)] for i in range(count)
    ]
    ambient = 0.5 * jnp.full((SUBLANES, LANES), transfer[7], jnp.float32)
    spread = (1.0 - ambient) / 3.0

    def band(r, carry):
        here = pl.ds(pl.multiple_of(r * SUBLANES, SUBLANES), SUBLANES)
        for x in range(width // LANES):
            at = pl.ds(x * LANES, LANES)
            shade = tinted = log_t = jnp.zeros((SUBLANES, LANES), jnp.float32)
            logs = [part[2, here, at] for part in parts]
            for i, part in enumerate(parts):
                ahead = sum(logs[j] * nearer[i][j] for j in range(count) if j != i)
                passing = jnp.exp2(ahead)
                shade = shade + passing * part[0, here, at]
                tinted = tinted + passing * part[1, here, at]
                log_t = log_t + logs[i]
            half = jnp.tanh(log_t * (-0.5 * LN2))
            opacity = (half + half) / (1.0 + half)
            full = ambient * opacity + spread * shade
            mixed = 0.5 * (full + ambient * tinted)
            for color in range(3):
                out[color, here, at] = transfer[color] * full + transfer[3 + color] * mixed
            out[3, here, at] = opacity
        return carry

    lax.fori_loop(0, rows // SUBLANES, band, 0)


def merge(parts, shifts, transfer):
    _, rows, width = parts[0].shape
    return pl.pallas_call(
        functools.partial(merge_kernel, shifts),
        in_specs=[SMEM] + [VMEM] * len(parts),
        out_specs=VMEM,
        out_shape=jax.ShapeDtypeStruct((4, rows, width), jnp.float32),
        compiler_params=pltpu.CompilerParams(vmem_limit_bytes=16 << 20),
        name="merge",
    )(transfer, *parts)


def on_device(volume, transfer):
    slices, rows, columns = volume.shape
    groups = lax.axis_size("depth")
    total_slices = slices * groups
    width = columns // groups
    first, last, top, bottom = cut(volume)
    edges = (
        pass_on(last, "depth", True),
        pass_on(first, "depth", False),
        pass_on(bottom, "row", True),
        pass_on(top, "row", False),
    )
    half = slices // 2
    halves = [(0, half + 1, 0, rows), (half + 1, slices - half - 1, 0, rows)]
    ring = [
        (0, slices, 0, 2 * SUBLANES),
        (0, slices, rows - 2 * SUBLANES, 2 * SUBLANES),
        (0, 2, 2 * SUBLANES, rows - 4 * SUBLANES),
        (slices - 2, 2, 2 * SUBLANES, rows - 4 * SUBLANES),
    ]
    shifts = order_of_shifts(groups)
    parts = []
    for stage, shift in enumerate(shifts):
        if stage == 0:
            kernel = functools.partial(inner_kernel, shift, halves, total_slices)
            inner = render(kernel, halves, transfer, volume, (), width, False)
            kernel = functools.partial(rest_kernel, shift, ring, total_slices)
            part = render(kernel, ring, transfer, volume, edges + (inner,), width, True)
        else:
            kernel = functools.partial(full_kernel, shift, 8, halves, total_slices)
            part = render(kernel, halves, transfer, volume, edges, width, True)
        if shift:
            pairs = [(i, (i + shift) % groups) for i in range(groups)]
            part = lax.ppermute(part, "depth", pairs)
        parts.append(part)
    return merge(parts, shifts, transfer)


def order_of_shifts(groups):
    return sorted(range(1, groups), key=lambda s: -min(s, groups - s)) + [0]


def solution(mesh):
    in_specs = (P("depth", "row", None), P())
    out_specs = P(None, "row", "depth")

    return jax.shard_map(
        on_device, mesh=mesh, in_specs=in_specs, out_specs=out_specs, check_vma=False
    )
```

```python
import functools
import math

import jax
import jax.numpy as jnp
from jax import lax
from jax.experimental import pallas as pl
from jax.experimental.pallas import tpu as pltpu
from jax.sharding import PartitionSpec as P


LANES = 128
SUBLANES = 8
LN2 = math.log(2.0)
SMEM = pl.BlockSpec(memory_space=pltpu.SMEM)
VMEM = pl.BlockSpec(memory_space=pltpu.VMEM)
ANY = pl.BlockSpec(memory_space=pl.ANY)


def cut_kernel(volume, first, last, top, bottom, sems):
    slices, rows, _ = volume.shape
    copies = [
        pltpu.make_async_copy(source, target, sems.at[i])
        for i, (source, target) in enumerate(
            [
                (volume.at[pl.ds(0, 1)], first),
                (volume.at[pl.ds(slices - 1, 1)], last),
                (volume.at[:, pl.ds(0, 1), :], top),
                (volume.at[:, pl.ds(rows - 1, 1), :], bottom),
            ]
        )
    ]
    for copy in copies:
        copy.start()
    for copy in copies:
        copy.wait()


def cut(volume):
    slices, rows, columns = volume.shape
    slab = jax.ShapeDtypeStruct((1, rows, columns), jnp.float32)
    strip = jax.ShapeDtypeStruct((slices, 1, columns), jnp.float32)
    return pl.pallas_call(
        cut_kernel,
        in_specs=[ANY],
        out_specs=[VMEM] * 4,
        out_shape=[slab, slab, strip, strip],
        scratch_shapes=[pltpu.SemaphoreType.DMA((4,))],
        name="cut",
    )(volume)


def pass_on(value, axis, forward):
    count = lax.axis_size(axis)
    pairs = [(i, i + 1) if forward else (i + 1, i) for i in range(count - 1)]
    return lax.ppermute(value, axis, pairs)


def tile_constants():
    lane = lax.broadcasted_iota(jnp.int32, (SUBLANES, LANES), 1)
    return lane == 0, lane == LANES - 1


def coefficients(transfer, slices):
    gamma = jnp.full((SUBLANES, LANES), transfer[6], jnp.float32) * (-2.0 / slices)
    ambient = 0.5 * jnp.full((SUBLANES, LANES), transfer[7], jnp.float32)
    return gamma, (1.0 - ambient) / (3.0 * ambient)


def cell(cells, c, z, row, x, below, above, state, coef, ends):
    log_t, passing, shade, tinted = state
    gamma, ratio = coef
    first, last = ends
    here = pl.ds(row, SUBLANES)
    right = cells[c + 1, z, here, :]
    left = cells[c - 1, z, here, :]
    d_row = cells[c, z, pl.ds(row + 1, SUBLANES), :] - cells[c, z, pl.ds(row - 1, SUBLANES), :]
    to_right = pltpu.roll(jnp.where(first, right, x), LANES - 1, 1)
    to_left = pltpu.roll(jnp.where(last, left, x), 1, 1)
    d_col = to_right - to_left
    d_depth = above - below
    plane = d_row + d_col
    along = d_depth + (plane + plane)
    norm = d_depth * d_depth + (d_row * d_row + (d_col * d_col + 4.0))
    lambert = jnp.abs(along) * lax.rsqrt(norm)
    log_t = log_t + gamma * jnp.log2(1.0 + jnp.exp(x))
    after = jnp.exp2(log_t)
    taken = passing - after
    lit = taken * lambert
    shade = shade + lit
    tinted = tinted + (taken + ratio * lit) * jnp.tanh(x)
    return log_t, after, shade, tinted


def fresh_state():
    zero = jnp.zeros((SUBLANES, LANES), jnp.float32)
    return zero, jnp.ones((SUBLANES, LANES), jnp.float32), zero, zero


def put(out, c, row, state):
    log_t, _, shade, tinted = state
    rows = pl.ds(row - SUBLANES, SUBLANES)
    lanes = pl.ds((c - 1) * LANES, LANES)
    if not isinstance(row, int):
        rows = pl.ds(pl.multiple_of(row - SUBLANES, SUBLANES), SUBLANES)
    if not isinstance(c, int):
        lanes = pl.ds(pl.multiple_of((c - 1) * LANES, LANES), LANES)
    for channel, value in enumerate((shade, tinted, log_t)):
        out[channel, rows, lanes] = value


class Bricks:
    def __init__(self, volume, cells, sems, flip, chunks, pieces):
        self.volume, self.cells, self.sems, self.pieces = volume, cells, sems, pieces
        self.chunks = chunks
        self.total = volume.shape[2] // LANES
        block = lax.bitwise_xor(lax.axis_index("depth"), jnp.int32(flip))
        self.base = block * chunks
        self.has_left = self.base > 0
        self.has_right = self.base + chunks < self.total

    def lanes(self, c):
        at = jnp.clip(self.base + (c - 1), 0, self.total - 1)
        return pl.ds(pl.multiple_of(at * LANES, LANES), LANES)

    def copy(self, c, k):
        z, depth, y, height = self.pieces[k]
        return pltpu.make_async_copy(
            self.volume.at[pl.ds(z, depth), pl.ds(y, height), self.lanes(c)],
            self.cells.at[c, pl.ds(z + 1, depth), pl.ds(y + SUBLANES, height), :],
            self.sems.at[c, k],
        )

    def clear(self, c):
        slices, rows, _ = self.volume.shape
        zero = jnp.zeros((SUBLANES, LANES), jnp.float32)

        def slice_of(z, carry):
            for r in range(rows // SUBLANES):
                self.cells[c, z + 1, pl.ds(SUBLANES * (r + 1), SUBLANES), :] = zero
            return carry

        lax.fori_loop(0, slices, slice_of, 0)

    def start(self, k, chunks):
        for c in chunks:
            if c == 0:
                pl.when(self.has_left)(lambda: self.copy(0, k).start())
            elif c == self.chunks + 1:
                pl.when(self.has_right)(lambda: self.copy(self.chunks + 1, k).start())
            else:
                self.copy(c, k).start()

    def start_all(self):
        for k in range(len(self.pieces)):
            self.start(k, (1, 0, 2))
        for c in range(3, self.chunks + 2):
            for k in range(len(self.pieces)):
                self.start(k, (c,))
        pl.when(jnp.logical_not(self.has_left))(lambda: self.clear(0))
        pl.when(jnp.logical_not(self.has_right))(lambda: self.clear(self.chunks + 1))

    def land(self, c, k):
        @pl.when(c == 1)
        def _():
            self.copy(1, k).wait()
            self.copy(2, k).wait()
            pl.when(self.has_left)(lambda: self.copy(0, k).wait())

        @pl.when(jnp.logical_and(c > 1, jnp.logical_or(c < self.chunks, self.has_right)))
        def _():
            self.copy(c + 1, k).wait()


def edge_copies(bricks, edges, sems, c):
    before, after, above_row, below_row = edges
    slices, rows, _ = bricks.volume.shape
    cells, at = bricks.cells, bricks.lanes(c)
    inner = pl.ds(SUBLANES, rows)
    middle = pl.ds(1, slices)
    pairs = [
        (before.at[0, :, at], cells.at[c, 0, inner, :]),
        (after.at[0, :, at], cells.at[c, slices + 1, inner, :]),
        (above_row.at[:, :, at], cells.at[c, middle, pl.ds(SUBLANES - 1, 1), :]),
        (below_row.at[:, :, at], cells.at[c, middle, pl.ds(SUBLANES + rows, 1), :]),
    ]
    return [pltpu.make_async_copy(*pair, sems.at[c, i]) for i, pair in enumerate(pairs)]


def march(cells, c, rows, begin, step, trips, coef, ends, arrive):
    def at(z):
        return [cells[c, z, pl.ds(row, SUBLANES), :] for row in rows]

    def trip(k, carry):
        arrive(k)
        states, belows, centers = carry
        for i in range(step):
            z = begin + 1 + k * step + i
            aboves = at(z + 1)
            states = [
                cell(cells, c, z, *tile, coef, ends)
                for tile in zip(rows, centers, belows, aboves, states)
            ]
            belows, centers = centers, aboves
        return states, belows, centers

    carry = ([fresh_state()] * len(rows), at(begin), at(begin + 1))
    if trips == 1:
        return trip(0, carry)[0]
    return lax.fori_loop(0, trips, trip, carry)[0]


def full_kernel(flip, tiles, pieces, total_slices, transfer, volume, *refs):
    *edges, out, cells, sems, edge_sems = refs
    slices, rows, _ = volume.shape
    chunks = out.shape[2] // LANES
    trips = len(pieces)
    groups = rows // SUBLANES // tiles
    bricks = Bricks(volume, cells, sems, flip, chunks, pieces)
    for copy in edge_copies(bricks, edges, edge_sems, 1):
        copy.start()
    bricks.start_all()
    for c in range(2, chunks + 1):
        for copy in edge_copies(bricks, edges, edge_sems, c):
            copy.start()
    coef = coefficients(transfer, total_slices)
    ends = tile_constants()

    def group(index, carry):
        c = index // groups + 1
        row = pl.multiple_of((index % groups * tiles + 1) * SUBLANES, SUBLANES)
        fresh = index % groups == 0

        @pl.when(fresh)
        def _():
            for copy in edge_copies(bricks, edges, edge_sems, c):
                copy.wait()
            bricks.land(c, 0)

        def arrive(k):
            for part in range(1, trips):
                pl.when(jnp.logical_and(fresh, k == part))(lambda part=part: bricks.land(c, part))

        at_rows = [row + SUBLANES * t for t in range(tiles)]
        states = march(cells, c, at_rows, 0, slices // trips, trips, coef, ends, arrive)
        for at_row, state in zip(at_rows, states):
            put(out, c, at_row, state)
        return carry

    lax.fori_loop(0, chunks * groups, group, 0)


def inner_kernel(flip, pieces, total_slices, transfer, volume, out, cells, sems):
    slices, rows, _ = volume.shape
    chunks = out.shape[2] // LANES
    trips = len(pieces)
    bricks = Bricks(volume, cells, sems, flip, chunks, pieces)
    bricks.start_all()
    coef = coefficients(transfer, total_slices)
    ends = tile_constants()
    at_rows = [SUBLANES * (t + 2) for t in range(rows // SUBLANES - 2)]

    def group(index, carry):
        c = index + 1
        bricks.land(c, 0)

        def arrive(k):
            for part in range(1, trips):
                pl.when(k == part)(lambda part=part: bricks.land(c, part))

        states = march(
            cells, c, at_rows, 1, (slices - 2) // trips, trips, coef, ends, arrive
        )
        for at_row, state in zip(at_rows, states):
            put(out, c, at_row, state)
        return carry

    lax.fori_loop(0, chunks, group, 0)


def rest_kernel(flip, pieces, total_slices, transfer, volume, *refs):
    *edges, inner, out, cells, sems, edge_sems = refs
    slices, rows, _ = volume.shape
    chunks = out.shape[2] // LANES
    bricks = Bricks(volume, cells, sems, flip, chunks, pieces)
    for copy in edge_copies(bricks, edges, edge_sems, 1):
        copy.start()
    bricks.start_all()
    for c in range(2, chunks + 1):
        for copy in edge_copies(bricks, edges, edge_sems, c):
            copy.start()
    coef = coefficients(transfer, total_slices)
    ends = tile_constants()

    def group(index, carry):
        c = index + 1
        for copy in edge_copies(bricks, edges, edge_sems, c):
            copy.wait()
        for k in range(len(pieces)):
            bricks.land(c, k)
        outer = [SUBLANES, rows]
        states = march(cells, c, outer, 0, slices, 1, coef, ends, lambda k: None)
        for at_row, state in zip(outer, states):
            put(out, c, at_row, state)
        lanes = pl.ds(pl.multiple_of((c - 1) * LANES, LANES), LANES)
        for t in range(1, rows // SUBLANES - 1):
            row = SUBLANES * (t + 1)
            here = pl.ds(row, SUBLANES)
            sides = []
            for z in (1, slices):
                below, x, above = [cells[c, z + i, here, :] for i in (-1, 0, 1)]
                sides.append(cell(cells, c, z, row, x, below, above, fresh_state(), coef, ends))
            (log_a, pass_a, shade_a, tint_a), (log_b, _, shade_b, tint_b) = sides
            shade, tint, log_t = [inner[i, pl.ds(row - SUBLANES, SUBLANES), lanes] for i in range(3)]
            passing = jnp.exp2(log_t)
            shade = shade_a + pass_a * (shade + passing * shade_b)
            tint = tint_a + pass_a * (tint + passing * tint_b)
            put(out, c, row, (log_a + log_t + log_b, None, shade, tint))
        return carry

    lax.fori_loop(0, chunks, group, 0)


def render(kernel, pieces, transfer, volume, extra, width, halo):
    slices, rows, _ = volume.shape
    chunks = width // LANES
    scratch = [
        pltpu.VMEM((chunks + 2, slices + 2, rows + 2 * SUBLANES, LANES), jnp.float32),
        pltpu.SemaphoreType.DMA((chunks + 2, len(pieces))),
    ]
    if halo:
        scratch.append(pltpu.SemaphoreType.DMA((chunks + 1, 4)))
    return pl.pallas_call(
        kernel,
        in_specs=[SMEM, ANY] + [ANY] * min(4, len(extra)) + [VMEM] * (len(extra) - 4),
        out_specs=VMEM,
        out_shape=jax.ShapeDtypeStruct((3, rows, width), jnp.float32),
        scratch_shapes=scratch,
        compiler_params=pltpu.CompilerParams(vmem_limit_bytes=32 << 20),
    )(transfer, volume, *extra)


def merge_kernel(flips, transfer, *refs):
    *parts, out = refs
    count = len(parts)
    mine = lax.axis_index("depth")
    rows, width = out.shape[1:]
    sources = [lax.bitwise_xor(mine, jnp.int32(flip)) for flip in flips]
    nearer = [
        [jnp.where(sources[j] < sources[i], 1.0, 0.0) for j in range(count)] for i in range(count)
    ]
    ambient = 0.5 * jnp.full((SUBLANES, LANES), transfer[7], jnp.float32)
    spread = (1.0 - ambient) / 3.0

    def band(r, carry):
        here = pl.ds(pl.multiple_of(r * SUBLANES, SUBLANES), SUBLANES)
        for x in range(width // LANES):
            at = pl.ds(x * LANES, LANES)
            shade = tinted = log_t = jnp.zeros((SUBLANES, LANES), jnp.float32)
            logs = [part[2, here, at] for part in parts]
            for i, part in enumerate(parts):
                ahead = sum(logs[j] * nearer[i][j] for j in range(count) if j != i)
                passing = jnp.exp2(ahead)
                shade = shade + passing * part[0, here, at]
                tinted = tinted + passing * part[1, here, at]
                log_t = log_t + logs[i]
            half = jnp.tanh(log_t * (-0.5 * LN2))
            opacity = (half + half) / (1.0 + half)
            full = ambient * opacity + spread * shade
            mixed = 0.5 * (full + ambient * tinted)
            for color in range(3):
                out[color, here, at] = transfer[color] * full + transfer[3 + color] * mixed
            out[3, here, at] = opacity
        return carry

    lax.fori_loop(0, rows // SUBLANES, band, 0)


def merge(parts, flips, transfer):
    _, rows, width = parts[0].shape
    return pl.pallas_call(
        functools.partial(merge_kernel, flips),
        in_specs=[SMEM] + [VMEM] * len(parts),
        out_specs=VMEM,
        out_shape=jax.ShapeDtypeStruct((4, rows, width), jnp.float32),
        compiler_params=pltpu.CompilerParams(vmem_limit_bytes=16 << 20),
        name="merge",
    )(transfer, *parts)


def fold_kernel(own, passed, out):
    rows, width = out.shape[1:]
    from_front = lax.axis_index("depth") < lax.axis_size("depth") // 2

    def band(r, carry):
        here = pl.ds(pl.multiple_of(r * SUBLANES, SUBLANES), SUBLANES)
        for x in range(width // LANES):
            at = pl.ds(x * LANES, LANES)
            log_own, log_passed = own[2, here, at], passed[2, here, at]
            passing = jnp.exp2(jnp.where(from_front, log_passed, log_own))
            for channel in range(2):
                a, b = own[channel, here, at], passed[channel, here, at]
                front, back = jnp.where(from_front, b, a), jnp.where(from_front, a, b)
                out[channel, here, at] = front + passing * back
            out[2, here, at] = log_own + log_passed
        return carry

    lax.fori_loop(0, rows // SUBLANES, band, 0)


def fold(own, passed):
    return pl.pallas_call(
        fold_kernel,
        in_specs=[VMEM, VMEM],
        out_specs=VMEM,
        out_shape=jax.ShapeDtypeStruct(own.shape, jnp.float32),
        compiler_params=pltpu.CompilerParams(vmem_limit_bytes=16 << 20),
        name="fold",
    )(own, passed)


def exchange(part, groups, flip, members=None):
    pairs = [(i, i ^ flip) for i in range(groups) if members is None or i in members]
    return lax.ppermute(part, "depth", pairs)


def on_device(volume, transfer):
    slices, rows, columns = volume.shape
    groups = lax.axis_size("depth")
    total_slices = slices * groups
    width = columns // groups
    first, last, top, bottom = cut(volume)
    edges = (
        pass_on(last, "depth", True),
        pass_on(first, "depth", False),
        pass_on(bottom, "row", True),
        pass_on(top, "row", False),
    )
    half = slices // 2
    halves = [(0, half + 1, 0, rows), (half + 1, slices - half - 1, 0, rows)]
    ring = [
        (0, slices, 0, SUBLANES),
        (2, slices - 4, SUBLANES, 1),
        (2, slices - 4, rows - SUBLANES - 1, 1),
        (0, slices, rows - SUBLANES, SUBLANES),
        (0, 2, SUBLANES, rows - 2 * SUBLANES),
        (slices - 2, 2, SUBLANES, rows - 2 * SUBLANES),
    ]
    flips = list(range(groups - 1, -1, -1))
    hop = groups == 4
    parts = []
    for stage, flip in enumerate(flips):
        if stage == 0:
            kernel = functools.partial(inner_kernel, flip, halves, total_slices)
            inner = render(kernel, halves, transfer, volume, (), width, False)
            kernel = functools.partial(rest_kernel, flip, ring, total_slices)
            part = render(kernel, ring, transfer, volume, edges + (inner,), width, True)
        else:
            kernel = functools.partial(full_kernel, flip, 8, halves, total_slices)
            part = render(kernel, halves, transfer, volume, edges, width, True)
        if hop and stage == 0:
            passed = lax.ppermute(part, "depth", [(0, 1), (3, 2)])
            part = exchange(part, groups, flip, (1, 2))
        elif flip:
            if hop and stage == 1:
                part = fold(part, passed)
            part = exchange(part, groups, flip)
        parts.append(part)
    return merge(parts, flips, transfer)


def solution(mesh):
    in_specs = (P("depth", "row", None), P())
    out_specs = P(None, "row", "depth")

    return jax.shard_map(
        on_device, mesh=mesh, in_specs=in_specs, out_specs=out_specs, check_vma=False
    )
```

```python
import functools
import math

import jax
import jax.numpy as jnp
from jax import lax
from jax.experimental import pallas as pl
from jax.experimental.pallas import tpu as pltpu
from jax.sharding import PartitionSpec as P


LANES = 128
SUBLANES = 8
LN2 = math.log(2.0)
SMEM = pl.BlockSpec(memory_space=pltpu.SMEM)
VMEM = pl.BlockSpec(memory_space=pltpu.VMEM)
ANY = pl.BlockSpec(memory_space=pl.ANY)


def cut_kernel(volume, first, last, top, bottom, sems):
    slices, rows, _ = volume.shape
    copies = [
        pltpu.make_async_copy(source, target, sems.at[i])
        for i, (source, target) in enumerate(
            [
                (volume.at[pl.ds(0, 1)], first),
                (volume.at[pl.ds(slices - 1, 1)], last),
                (volume.at[:, pl.ds(0, 1), :], top),
                (volume.at[:, pl.ds(rows - 1, 1), :], bottom),
            ]
        )
    ]
    for copy in copies:
        copy.start()
    for copy in copies:
        copy.wait()


def cut(volume):
    slices, rows, columns = volume.shape
    slab = jax.ShapeDtypeStruct((1, rows, columns), jnp.float32)
    strip = jax.ShapeDtypeStruct((slices, 1, columns), jnp.float32)
    return pl.pallas_call(
        cut_kernel,
        in_specs=[ANY],
        out_specs=[VMEM] * 4,
        out_shape=[slab, slab, strip, strip],
        scratch_shapes=[pltpu.SemaphoreType.DMA((4,))],
        name="cut",
    )(volume)


def pass_on(value, axis, forward):
    count = lax.axis_size(axis)
    pairs = [(i, i + 1) if forward else (i + 1, i) for i in range(count - 1)]
    return lax.ppermute(value, axis, pairs)


def tile_constants():
    lane = lax.broadcasted_iota(jnp.int32, (SUBLANES, LANES), 1)
    return lane == 0, lane == LANES - 1


def coefficients(transfer, slices):
    gamma = jnp.full((SUBLANES, LANES), transfer[6], jnp.float32) * (-2.0 / slices)
    ambient = 0.5 * jnp.full((SUBLANES, LANES), transfer[7], jnp.float32)
    return gamma, (1.0 - ambient) / (3.0 * ambient)


def cell(cells, c, z, row, x, below, above, state, coef, ends):
    log_t, passing, shade, tinted = state
    gamma, ratio = coef
    first, last = ends
    here = pl.ds(row, SUBLANES)
    right = cells[c + 1, z, here, :]
    left = cells[c - 1, z, here, :]
    d_row = cells[c, z, pl.ds(row + 1, SUBLANES), :] - cells[c, z, pl.ds(row - 1, SUBLANES), :]
    to_right = pltpu.roll(jnp.where(first, right, x), LANES - 1, 1)
    to_left = pltpu.roll(jnp.where(last, left, x), 1, 1)
    d_col = to_right - to_left
    d_depth = above - below
    plane = d_row + d_col
    along = d_depth + (plane + plane)
    norm = d_depth * d_depth + (d_row * d_row + (d_col * d_col + 4.0))
    lambert = jnp.abs(along) * lax.rsqrt(norm)
    log_t = log_t + gamma * jnp.log2(1.0 + jnp.exp(x))
    after = jnp.exp2(log_t)
    taken = passing - after
    lit = taken * lambert
    shade = shade + lit
    tinted = tinted + (taken + ratio * lit) * jnp.tanh(x)
    return log_t, after, shade, tinted


def fresh_state():
    zero = jnp.zeros((SUBLANES, LANES), jnp.float32)
    return zero, jnp.ones((SUBLANES, LANES), jnp.float32), zero, zero


def put(out, c, row, state):
    log_t, _, shade, tinted = state
    rows = pl.ds(row - SUBLANES, SUBLANES)
    lanes = pl.ds((c - 1) * LANES, LANES)
    if not isinstance(row, int):
        rows = pl.ds(pl.multiple_of(row - SUBLANES, SUBLANES), SUBLANES)
    if not isinstance(c, int):
        lanes = pl.ds(pl.multiple_of((c - 1) * LANES, LANES), LANES)
    for channel, value in enumerate((shade, tinted, log_t)):
        out[channel, rows, lanes] = value


class Bricks:
    def __init__(self, volume, cells, sems, shift, chunks, pieces):
        self.volume, self.cells, self.sems, self.pieces = volume, cells, sems, pieces
        self.chunks = chunks
        self.total = volume.shape[2] // LANES
        block = lax.rem(lax.axis_index("depth") + shift, lax.axis_size("depth"))
        self.base = block * chunks
        self.has_left = self.base > 0
        self.has_right = self.base + chunks < self.total

    def lanes(self, c):
        at = jnp.clip(self.base + (c - 1), 0, self.total - 1)
        return pl.ds(pl.multiple_of(at * LANES, LANES), LANES)

    def copy(self, c, k):
        z, depth, y, height = self.pieces[k]
        return pltpu.make_async_copy(
            self.volume.at[pl.ds(z, depth), pl.ds(y, height), self.lanes(c)],
            self.cells.at[c, pl.ds(z + 1, depth), pl.ds(y + SUBLANES, height), :],
            self.sems.at[c, k],
        )

    def clear(self, c):
        slices, rows, _ = self.volume.shape
        zero = jnp.zeros((SUBLANES, LANES), jnp.float32)

        def slice_of(z, carry):
            for r in range(rows // SUBLANES):
                self.cells[c, z + 1, pl.ds(SUBLANES * (r + 1), SUBLANES), :] = zero
            return carry

        lax.fori_loop(0, slices, slice_of, 0)

    def start(self, k, chunks):
        for c in chunks:
            if c == 0:
                pl.when(self.has_left)(lambda: self.copy(0, k).start())
            elif c == self.chunks + 1:
                pl.when(self.has_right)(lambda: self.copy(self.chunks + 1, k).start())
            else:
                self.copy(c, k).start()

    def start_all(self):
        for k in range(len(self.pieces)):
            self.start(k, (1, 0, 2))
        for c in range(3, self.chunks + 2):
            for k in range(len(self.pieces)):
                self.start(k, (c,))
        pl.when(jnp.logical_not(self.has_left))(lambda: self.clear(0))
        pl.when(jnp.logical_not(self.has_right))(lambda: self.clear(self.chunks + 1))

    def land(self, c, k):
        @pl.when(c == 1)
        def _():
            self.copy(1, k).wait()
            self.copy(2, k).wait()
            pl.when(self.has_left)(lambda: self.copy(0, k).wait())

        @pl.when(jnp.logical_and(c > 1, jnp.logical_or(c < self.chunks, self.has_right)))
        def _():
            self.copy(c + 1, k).wait()


class Edges:
    def __init__(self, bricks, sems, slabs, strips, spans):
        self.bricks, self.sems, self.slabs, self.strips, self.spans = bricks, sems, slabs, strips, spans

    def copies(self, c):
        slices, rows, _ = self.bricks.volume.shape
        cells, at = self.bricks.cells, self.bricks.lanes(c)
        pairs = []
        for slab, z in zip(self.slabs, (0, slices + 1)):
            pairs.append((slab.at[0, :, at], cells.at[c, z, pl.ds(SUBLANES, rows), :]))
        for strip, row in zip(self.strips, (SUBLANES - 1, SUBLANES + rows)):
            for z, size in self.spans:
                pairs.append(
                    (strip.at[pl.ds(z, size), :, at], cells.at[c, pl.ds(z + 1, size), pl.ds(row, 1), :])
                )
        return [pltpu.make_async_copy(*pair, self.sems.at[c, i]) for i, pair in enumerate(pairs)]

    def start(self, c):
        for copy in self.copies(c):
            copy.start()

    def wait(self, c):
        for copy in self.copies(c):
            copy.wait()


def start_everything(bricks, edges):
    edges.start(1)
    bricks.start_all()
    for c in range(2, bricks.chunks + 1):
        edges.start(c)


def march(cells, c, rows, begin, step, trips, coef, ends, arrive):
    def at(z):
        return [cells[c, z, pl.ds(row, SUBLANES), :] for row in rows]

    def trip(k, carry):
        arrive(k)
        states, belows, centers = carry
        for i in range(step):
            z = begin + 1 + k * step + i
            aboves = at(z + 1)
            states = [
                cell(cells, c, z, *tile, coef, ends)
                for tile in zip(rows, centers, belows, aboves, states)
            ]
            belows, centers = centers, aboves
        return states, belows, centers

    carry = ([fresh_state()] * len(rows), at(begin), at(begin + 1))
    if trips == 1:
        return trip(0, carry)[0]
    return lax.fori_loop(0, trips, trip, carry)[0]


def full_kernel(shift, tiles, pieces, total_slices, transfer, volume, *refs):
    before, after, above_row, below_row, out, cells, sems, edge_sems = refs
    slices, rows, _ = volume.shape
    chunks = out.shape[2] // LANES
    trips = len(pieces)
    groups = rows // SUBLANES // tiles
    bricks = Bricks(volume, cells, sems, shift, chunks, pieces)
    edges = Edges(bricks, edge_sems, (before, after), (above_row, below_row), [(0, slices)])
    start_everything(bricks, edges)
    coef = coefficients(transfer, total_slices)
    ends = tile_constants()

    def group(index, carry):
        c = index // groups + 1
        row = pl.multiple_of((index % groups * tiles + 1) * SUBLANES, SUBLANES)
        fresh = index % groups == 0

        @pl.when(fresh)
        def _():
            edges.wait(c)
            bricks.land(c, 0)

        def arrive(k):
            for part in range(1, trips):
                pl.when(jnp.logical_and(fresh, k == part))(lambda part=part: bricks.land(c, part))

        at_rows = [row + SUBLANES * t for t in range(tiles)]
        states = march(cells, c, at_rows, 0, slices // trips, trips, coef, ends, arrive)
        for at_row, state in zip(at_rows, states):
            put(out, c, at_row, state)
        return carry

    lax.fori_loop(0, chunks * groups, group, 0)


def inner_kernel(shift, pieces, total_slices, transfer, volume, out, cells, sems):
    slices, rows, _ = volume.shape
    chunks = out.shape[2] // LANES
    trips = len(pieces)
    bricks = Bricks(volume, cells, sems, shift, chunks, pieces)
    bricks.start_all()
    coef = coefficients(transfer, total_slices)
    ends = tile_constants()
    at_rows = [SUBLANES * (t + 2) for t in range(rows // SUBLANES - 2)]

    def group(index, carry):
        c = index + 1
        bricks.land(c, 0)

        def arrive(k):
            for part in range(1, trips):
                pl.when(k == part)(lambda part=part: bricks.land(c, part))

        states = march(
            cells, c, at_rows, 1, (slices - 2) // trips, trips, coef, ends, arrive
        )
        for at_row, state in zip(at_rows, states):
            put(out, c, at_row, state)
        return carry

    lax.fori_loop(0, chunks, group, 0)


def outer_kernel(shift, pieces, total_slices, transfer, volume, *refs):
    above_row, below_row, out, cells, sems, edge_sems = refs
    slices, rows, _ = volume.shape
    chunks = out.shape[2] // LANES
    bricks = Bricks(volume, cells, sems, shift, chunks, pieces)
    edges = Edges(bricks, edge_sems, (), (above_row, below_row), [(0, slices)])
    start_everything(bricks, edges)
    coef = coefficients(transfer, total_slices)
    ends = tile_constants()

    def group(index, carry):
        c = index + 1
        edges.wait(c)
        for k in range(len(pieces)):
            bricks.land(c, k)
        at_rows = [SUBLANES, rows]
        states = march(cells, c, at_rows, 1, slices - 2, 1, coef, ends, lambda k: None)
        for place, state in enumerate(states):
            put(out, c, SUBLANES * (place + 1), state)
        return carry

    lax.fori_loop(0, chunks, group, 0)


def close_kernel(shift, pieces, total_slices, transfer, volume, *refs):
    before, after, above_row, below_row, inner, outer, out, cells, sems, edge_sems = refs
    slices, rows, _ = volume.shape
    chunks = out.shape[2] // LANES
    tiles = rows // SUBLANES
    bricks = Bricks(volume, cells, sems, shift, chunks, pieces)
    spans = [(0, 1), (slices - 1, 1)]
    edges = Edges(bricks, edge_sems, (before, after), (above_row, below_row), spans)
    start_everything(bricks, edges)
    coef = coefficients(transfer, total_slices)
    ends = tile_constants()

    def group(index, carry):
        c = index + 1
        edges.wait(c)
        for k in range(len(pieces)):
            bricks.land(c, k)
        lanes = pl.ds(pl.multiple_of(index * LANES, LANES), LANES)
        for t in range(tiles):
            row = SUBLANES * (t + 1)
            here = pl.ds(row, SUBLANES)
            sides = []
            for z in (1, slices):
                below, x, above = [cells[c, z + i, here, :] for i in (-1, 0, 1)]
                sides.append(cell(cells, c, z, row, x, below, above, fresh_state(), coef, ends))
            (log_a, pass_a, shade_a, tint_a), (log_b, _, shade_b, tint_b) = sides
            between, place = (inner, t) if 0 < t < tiles - 1 else (outer, min(t, 1))
            held = pl.ds(SUBLANES * place, SUBLANES)
            shade, tint, log_t = [between[i, held, lanes] for i in range(3)]
            passing = jnp.exp2(log_t)
            shade = shade_a + pass_a * (shade + passing * shade_b)
            tint = tint_a + pass_a * (tint + passing * tint_b)
            put(out, c, row, (log_a + log_t + log_b, None, shade, tint))
        return carry

    lax.fori_loop(0, chunks, group, 0)


def render(kernel, pieces, transfer, volume, halo, done, width, out_rows=None):
    slices, rows, _ = volume.shape
    chunks = width // LANES
    scratch = [
        pltpu.VMEM((chunks + 2, slices + 2, rows + 2 * SUBLANES, LANES), jnp.float32),
        pltpu.SemaphoreType.DMA((chunks + 2, len(pieces))),
    ]
    if halo:
        scratch.append(pltpu.SemaphoreType.DMA((chunks + 1, 6)))
    return pl.pallas_call(
        functools.partial(kernel, pieces, slices * lax.axis_size("depth")),
        in_specs=[SMEM, ANY] + [ANY] * len(halo) + [VMEM] * len(done),
        out_specs=VMEM,
        out_shape=jax.ShapeDtypeStruct((3, out_rows or rows, width), jnp.float32),
        scratch_shapes=scratch,
        compiler_params=pltpu.CompilerParams(vmem_limit_bytes=32 << 20),
    )(transfer, volume, *halo, *done)


def merge_kernel(shifts, transfer, *refs):
    *parts, image, out, sems = refs
    count = len(parts)
    mine = lax.axis_index("depth")
    rows, width = out.shape[1:]
    sources = [lax.rem(mine - shift + count, count) for shift in shifts]
    nearer = [
        [jnp.where(sources[j] < sources[i], 1.0, 0.0) for j in range(count)] for i in range(count)
    ]
    ambient = 0.5 * jnp.full((SUBLANES, LANES), transfer[7], jnp.float32)
    spread = (1.0 - ambient) / 3.0

    def band(r, carry):
        here = pl.ds(pl.multiple_of(r * SUBLANES, SUBLANES), SUBLANES)
        for x in range(width // LANES):
            at = pl.ds(x * LANES, LANES)
            shade = tinted = log_t = jnp.zeros((SUBLANES, LANES), jnp.float32)
            logs = [part[2, here, at] for part in parts]
            for i, part in enumerate(parts):
                ahead = sum(logs[j] * nearer[i][j] for j in range(count) if j != i)
                passing = jnp.exp2(ahead)
                shade = shade + passing * part[0, here, at]
                tinted = tinted + passing * part[1, here, at]
                log_t = log_t + logs[i]
            half = jnp.tanh(log_t * (-0.5 * LN2))
            opacity = (half + half) / (1.0 + half)
            full = ambient * opacity + spread * shade
            mixed = 0.5 * (full + ambient * tinted)
            for color in range(3):
                out[color, here, at] = transfer[color] * full + transfer[3 + color] * mixed
            out[3, here, at] = opacity
        copy(r).start()
        return carry

    def copy(r):
        here = pl.ds(pl.multiple_of(r * SUBLANES, SUBLANES), SUBLANES)
        return pltpu.make_async_copy(out.at[:, here, :], image.at[:, here, :], sems.at[r])

    lax.fori_loop(0, rows // SUBLANES, band, 0)
    for r in range(rows // SUBLANES):
        copy(r).wait()


def merge(parts, shifts, transfer):
    _, rows, width = parts[0].shape
    return pl.pallas_call(
        functools.partial(merge_kernel, shifts),
        in_specs=[SMEM] + [VMEM] * len(parts),
        out_specs=ANY,
        out_shape=jax.ShapeDtypeStruct((4, rows, width), jnp.float32),
        scratch_shapes=[
            pltpu.VMEM((4, rows, width), jnp.float32),
            pltpu.SemaphoreType.DMA((rows // SUBLANES,)),
        ],
        compiler_params=pltpu.CompilerParams(vmem_limit_bytes=16 << 20),
        name="merge",
    )(transfer, *parts)


def on_device(volume, transfer):
    slices, rows, columns = volume.shape
    groups = lax.axis_size("depth")
    width = columns // groups
    first, last, top, bottom = cut(volume)
    slabs = (pass_on(last, "depth", True), pass_on(first, "depth", False))
    strips = (pass_on(bottom, "row", True), pass_on(top, "row", False))
    half = slices // 2
    halves = [(0, half + 1, 0, rows), (half + 1, slices - half - 1, 0, rows)]
    rim = [(0, slices, 0, 2 * SUBLANES), (0, slices, rows - 2 * SUBLANES, 2 * SUBLANES)]
    caps = [(0, 2, 0, rows), (slices - 2, 2, 0, rows)]
    shifts = order_of_shifts(groups)
    parts = []
    for stage, shift in enumerate(shifts):
        if stage == 0:
            kernel = functools.partial(inner_kernel, shift)
            inner = render(kernel, halves, transfer, volume, (), (), width)
            kernel = functools.partial(outer_kernel, shift)
            outer = render(kernel, rim, transfer, volume, strips, (), width, 2 * SUBLANES)
            kernel = functools.partial(close_kernel, shift)
            done = (inner, outer)
            part = render(kernel, caps, transfer, volume, slabs + strips, done, width)
        else:
            kernel = functools.partial(full_kernel, shift, 8)
            part = render(kernel, halves, transfer, volume, slabs + strips, (), width)
        if shift:
            pairs = [(i, (i + shift) % groups) for i in range(groups)]
            part = lax.ppermute(part, "depth", pairs)
        parts.append(part)
    return merge(parts, shifts, transfer)


def order_of_shifts(groups):
    return sorted(range(1, groups), key=lambda s: -min(s, groups - s)) + [0]


def solution(mesh):
    in_specs = (P("depth", "row", None), P())
    out_specs = P(None, "row", "depth")

    return jax.shard_map(
        on_device, mesh=mesh, in_specs=in_specs, out_specs=out_specs, check_vma=False
    )
```

```python
import functools
import math

import jax
import jax.numpy as jnp
from jax import lax
from jax.experimental import pallas as pl
from jax.experimental.pallas import tpu as pltpu
from jax.sharding import PartitionSpec as P


LANES = 128
SUBLANES = 8
LN2 = math.log(2.0)
SMEM = pl.BlockSpec(memory_space=pltpu.SMEM)
VMEM = pl.BlockSpec(memory_space=pltpu.VMEM)
ANY = pl.BlockSpec(memory_space=pl.ANY)


def cut_kernel(volume, first, last, top, bottom, sems):
    slices, rows, _ = volume.shape
    copies = [
        pltpu.make_async_copy(source, target, sems.at[i])
        for i, (source, target) in enumerate(
            [
                (volume.at[pl.ds(0, 1)], first),
                (volume.at[pl.ds(slices - 1, 1)], last),
                (volume.at[:, pl.ds(0, 1), :], top),
                (volume.at[:, pl.ds(rows - 1, 1), :], bottom),
            ]
        )
    ]
    for copy in copies:
        copy.start()
    for copy in copies:
        copy.wait()


def cut(volume):
    slices, rows, columns = volume.shape
    slab = jax.ShapeDtypeStruct((1, rows, columns), jnp.float32)
    strip = jax.ShapeDtypeStruct((slices, 1, columns), jnp.float32)
    return pl.pallas_call(
        cut_kernel,
        in_specs=[ANY],
        out_specs=[VMEM] * 4,
        out_shape=[slab, slab, strip, strip],
        scratch_shapes=[pltpu.SemaphoreType.DMA((4,))],
        name="cut",
    )(volume)


def pass_on(value, axis, forward):
    count = lax.axis_size(axis)
    pairs = [(i, i + 1) if forward else (i + 1, i) for i in range(count - 1)]
    return lax.ppermute(value, axis, pairs)


def tile_constants():
    lane = lax.broadcasted_iota(jnp.int32, (SUBLANES, LANES), 1)
    return lane == 0, lane == LANES - 1


def coefficients(transfer, slices):
    gamma = jnp.full((SUBLANES, LANES), transfer[6], jnp.float32) * (-2.0 / slices)
    ambient = 0.5 * jnp.full((SUBLANES, LANES), transfer[7], jnp.float32)
    return gamma, (1.0 - ambient) / (3.0 * ambient)


def cell(cells, c, z, row, x, below, above, state, coef, ends):
    log_t, passing, shade, tinted = state
    gamma, ratio = coef
    first, last = ends
    here = pl.ds(row, SUBLANES)
    right = cells[c + 1, z, here, :]
    left = cells[c - 1, z, here, :]
    d_row = cells[c, z, pl.ds(row + 1, SUBLANES), :] - cells[c, z, pl.ds(row - 1, SUBLANES), :]
    to_right = pltpu.roll(jnp.where(first, right, x), LANES - 1, 1)
    to_left = pltpu.roll(jnp.where(last, left, x), 1, 1)
    d_col = to_right - to_left
    d_depth = above - below
    plane = d_row + d_col
    along = d_depth + (plane + plane)
    norm = d_depth * d_depth + (d_row * d_row + (d_col * d_col + 4.0))
    lambert = jnp.abs(along) * lax.rsqrt(norm)
    log_t = log_t + gamma * jnp.log2(1.0 + jnp.exp(x))
    after = jnp.exp2(log_t)
    taken = passing - after
    lit = taken * lambert
    shade = shade + lit
    tinted = tinted + (taken + ratio * lit) * jnp.tanh(x)
    return log_t, after, shade, tinted


def fresh_state():
    zero = jnp.zeros((SUBLANES, LANES), jnp.float32)
    return zero, jnp.ones((SUBLANES, LANES), jnp.float32), zero, zero


def put(out, c, row, state):
    log_t, _, shade, tinted = state
    rows = pl.ds(row - SUBLANES, SUBLANES)
    lanes = pl.ds((c - 1) * LANES, LANES)
    if not isinstance(row, int):
        rows = pl.ds(pl.multiple_of(row - SUBLANES, SUBLANES), SUBLANES)
    if not isinstance(c, int):
        lanes = pl.ds(pl.multiple_of((c - 1) * LANES, LANES), LANES)
    for channel, value in enumerate((shade, tinted, log_t)):
        out[channel, rows, lanes] = value


class Bricks:
    def __init__(self, volume, cells, sems, flip, chunks, pieces):
        self.volume, self.cells, self.sems, self.pieces = volume, cells, sems, pieces
        self.chunks = chunks
        self.total = volume.shape[2] // LANES
        block = lax.bitwise_xor(lax.axis_index("depth"), jnp.int32(flip))
        self.base = block * chunks
        self.has_left = self.base > 0
        self.has_right = self.base + chunks < self.total

    def lanes(self, c):
        at = jnp.clip(self.base + (c - 1), 0, self.total - 1)
        return pl.ds(pl.multiple_of(at * LANES, LANES), LANES)

    def copy(self, c, k):
        z, depth, y, height = self.pieces[k]
        return pltpu.make_async_copy(
            self.volume.at[pl.ds(z, depth), pl.ds(y, height), self.lanes(c)],
            self.cells.at[c, pl.ds(z + 1, depth), pl.ds(y + SUBLANES, height), :],
            self.sems.at[c, k],
        )

    def clear(self, c):
        slices, rows, _ = self.volume.shape
        zero = jnp.zeros((SUBLANES, LANES), jnp.float32)

        def slice_of(z, carry):
            for r in range(rows // SUBLANES):
                self.cells[c, z + 1, pl.ds(SUBLANES * (r + 1), SUBLANES), :] = zero
            return carry

        lax.fori_loop(0, slices, slice_of, 0)

    def start(self, k, chunks):
        for c in chunks:
            if c == 0:
                pl.when(self.has_left)(lambda: self.copy(0, k).start())
            elif c == self.chunks + 1:
                pl.when(self.has_right)(lambda: self.copy(self.chunks + 1, k).start())
            else:
                self.copy(c, k).start()

    def start_all(self):
        for k in range(len(self.pieces)):
            self.start(k, (1, 0, 2))
        for c in range(3, self.chunks + 2):
            for k in range(len(self.pieces)):
                self.start(k, (c,))
        pl.when(jnp.logical_not(self.has_left))(lambda: self.clear(0))
        pl.when(jnp.logical_not(self.has_right))(lambda: self.clear(self.chunks + 1))

    def land(self, c, k):
        @pl.when(c == 1)
        def _():
            self.copy(1, k).wait()
            self.copy(2, k).wait()
            pl.when(self.has_left)(lambda: self.copy(0, k).wait())

        @pl.when(jnp.logical_and(c > 1, jnp.logical_or(c < self.chunks, self.has_right)))
        def _():
            self.copy(c + 1, k).wait()


def edge_copies(bricks, edges, sems, c):
    before, after, above_row, below_row = edges
    slices, rows, _ = bricks.volume.shape
    cells, at = bricks.cells, bricks.lanes(c)
    inner = pl.ds(SUBLANES, rows)
    middle = pl.ds(1, slices)
    pairs = [
        (before.at[0, :, at], cells.at[c, 0, inner, :]),
        (after.at[0, :, at], cells.at[c, slices + 1, inner, :]),
        (above_row.at[:, :, at], cells.at[c, middle, pl.ds(SUBLANES - 1, 1), :]),
        (below_row.at[:, :, at], cells.at[c, middle, pl.ds(SUBLANES + rows, 1), :]),
    ]
    return [pltpu.make_async_copy(*pair, sems.at[c, i]) for i, pair in enumerate(pairs)]


def march(cells, c, rows, begin, step, trips, coef, ends, arrive):
    def at(z):
        return [cells[c, z, pl.ds(row, SUBLANES), :] for row in rows]

    def trip(k, carry):
        arrive(k)
        states, belows, centers = carry
        for i in range(step):
            z = begin + 1 + k * step + i
            aboves = at(z + 1)
            states = [
                cell(cells, c, z, *tile, coef, ends)
                for tile in zip(rows, centers, belows, aboves, states)
            ]
            belows, centers = centers, aboves
        return states, belows, centers

    carry = ([fresh_state()] * len(rows), at(begin), at(begin + 1))
    if trips == 1:
        return trip(0, carry)[0]
    return lax.fori_loop(0, trips, trip, carry)[0]


def full_kernel(flip, tiles, pieces, total_slices, transfer, volume, *refs):
    *edges, out, cells, sems, edge_sems = refs
    slices, rows, _ = volume.shape
    chunks = out.shape[2] // LANES
    trips = len(pieces)
    groups = rows // SUBLANES // tiles
    bricks = Bricks(volume, cells, sems, flip, chunks, pieces)
    for copy in edge_copies(bricks, edges, edge_sems, 1):
        copy.start()
    bricks.start_all()
    for c in range(2, chunks + 1):
        for copy in edge_copies(bricks, edges, edge_sems, c):
            copy.start()
    coef = coefficients(transfer, total_slices)
    ends = tile_constants()

    def group(index, carry):
        c = index // groups + 1
        row = pl.multiple_of((index % groups * tiles + 1) * SUBLANES, SUBLANES)
        fresh = index % groups == 0

        @pl.when(fresh)
        def _():
            for copy in edge_copies(bricks, edges, edge_sems, c):
                copy.wait()
            bricks.land(c, 0)

        def arrive(k):
            for part in range(1, trips):
                pl.when(jnp.logical_and(fresh, k == part))(lambda part=part: bricks.land(c, part))

        at_rows = [row + SUBLANES * t for t in range(tiles)]
        states = march(cells, c, at_rows, 0, slices // trips, trips, coef, ends, arrive)
        for at_row, state in zip(at_rows, states):
            put(out, c, at_row, state)
        return carry

    lax.fori_loop(0, chunks * groups, group, 0)


def inner_kernel(flip, pieces, total_slices, transfer, volume, out, cells, sems):
    slices, rows, _ = volume.shape
    chunks = out.shape[2] // LANES
    trips = len(pieces)
    bricks = Bricks(volume, cells, sems, flip, chunks, pieces)
    bricks.start_all()
    coef = coefficients(transfer, total_slices)
    ends = tile_constants()
    at_rows = [SUBLANES * (t + 2) for t in range(rows // SUBLANES - 2)]

    def group(index, carry):
        c = index + 1
        bricks.land(c, 0)

        def arrive(k):
            for part in range(1, trips):
                pl.when(k == part)(lambda part=part: bricks.land(c, part))

        states = march(
            cells, c, at_rows, 1, (slices - 2) // trips, trips, coef, ends, arrive
        )
        for at_row, state in zip(at_rows, states):
            put(out, c, at_row, state)
        return carry

    lax.fori_loop(0, chunks, group, 0)


def rest_kernel(flip, pieces, total_slices, transfer, volume, *refs):
    *edges, inner, out, cells, sems, edge_sems = refs
    slices, rows, _ = volume.shape
    chunks = out.shape[2] // LANES
    bricks = Bricks(volume, cells, sems, flip, chunks, pieces)
    for copy in edge_copies(bricks, edges, edge_sems, 1):
        copy.start()
    bricks.start_all()
    for c in range(2, chunks + 1):
        for copy in edge_copies(bricks, edges, edge_sems, c):
            copy.start()
    coef = coefficients(transfer, total_slices)
    ends = tile_constants()

    def group(index, carry):
        c = index + 1
        for copy in edge_copies(bricks, edges, edge_sems, c):
            copy.wait()
        for k in range(len(pieces)):
            bricks.land(c, k)
        outer = [SUBLANES, rows]
        states = march(cells, c, outer, 0, slices, 1, coef, ends, lambda k: None)
        for at_row, state in zip(outer, states):
            put(out, c, at_row, state)
        lanes = pl.ds(pl.multiple_of((c - 1) * LANES, LANES), LANES)
        for t in range(1, rows // SUBLANES - 1):
            row = SUBLANES * (t + 1)
            here = pl.ds(row, SUBLANES)
            sides = []
            for z in (1, slices):
                below, x, above = [cells[c, z + i, here, :] for i in (-1, 0, 1)]
                sides.append(cell(cells, c, z, row, x, below, above, fresh_state(), coef, ends))
            (log_a, pass_a, shade_a, tint_a), (log_b, _, shade_b, tint_b) = sides
            shade, tint, log_t = [inner[i, pl.ds(row - SUBLANES, SUBLANES), lanes] for i in range(3)]
            passing = jnp.exp2(log_t)
            shade = shade_a + pass_a * (shade + passing * shade_b)
            tint = tint_a + pass_a * (tint + passing * tint_b)
            put(out, c, row, (log_a + log_t + log_b, None, shade, tint))
        return carry

    lax.fori_loop(0, chunks, group, 0)


def render(kernel, pieces, transfer, volume, extra, width, halo):
    slices, rows, _ = volume.shape
    chunks = width // LANES
    scratch = [
        pltpu.VMEM((chunks + 2, slices + 2, rows + 2 * SUBLANES, LANES), jnp.float32),
        pltpu.SemaphoreType.DMA((chunks + 2, len(pieces))),
    ]
    if halo:
        scratch.append(pltpu.SemaphoreType.DMA((chunks + 1, 4)))
    return pl.pallas_call(
        kernel,
        in_specs=[SMEM, ANY] + [ANY] * min(4, len(extra)) + [VMEM] * (len(extra) - 4),
        out_specs=VMEM,
        out_shape=jax.ShapeDtypeStruct((3, rows, width), jnp.float32),
        scratch_shapes=scratch,
        compiler_params=pltpu.CompilerParams(vmem_limit_bytes=32 << 20),
    )(transfer, volume, *extra)


def merge_kernel(flips, transfer, *refs):
    *parts, out = refs
    count = len(parts)
    mine = lax.axis_index("depth")
    rows, width = out.shape[1:]
    sources = [lax.bitwise_xor(mine, jnp.int32(flip)) for flip in flips]
    nearer = [
        [jnp.where(sources[j] < sources[i], 1.0, 0.0) for j in range(count)] for i in range(count)
    ]
    ambient = 0.5 * jnp.full((SUBLANES, LANES), transfer[7], jnp.float32)
    spread = (1.0 - ambient) / 3.0

    def band(r, carry):
        here = pl.ds(pl.multiple_of(r * SUBLANES, SUBLANES), SUBLANES)
        for x in range(width // LANES):
            at = pl.ds(x * LANES, LANES)
            shade = tinted = log_t = jnp.zeros((SUBLANES, LANES), jnp.float32)
            logs = [part[2, here, at] for part in parts]
            for i, part in enumerate(parts):
                ahead = sum(logs[j] * nearer[i][j] for j in range(count) if j != i)
                passing = jnp.exp2(ahead)
                shade = shade + passing * part[0, here, at]
                tinted = tinted + passing * part[1, here, at]
                log_t = log_t + logs[i]
            half = jnp.tanh(log_t * (-0.5 * LN2))
            opacity = (half + half) / (1.0 + half)
            full = ambient * opacity + spread * shade
            mixed = 0.5 * (full + ambient * tinted)
            for color in range(3):
                out[color, here, at] = transfer[color] * full + transfer[3 + color] * mixed
            out[3, here, at] = opacity
        return carry

    lax.fori_loop(0, rows // SUBLANES, band, 0)


def merge(parts, flips, transfer):
    _, rows, width = parts[0].shape
    return pl.pallas_call(
        functools.partial(merge_kernel, flips),
        in_specs=[SMEM] + [VMEM] * len(parts),
        out_specs=VMEM,
        out_shape=jax.ShapeDtypeStruct((4, rows, width), jnp.float32),
        compiler_params=pltpu.CompilerParams(vmem_limit_bytes=16 << 20),
        name="merge",
    )(transfer, *parts)


def fold_kernel(lower_half, own, passed, out):
    rows, width = out.shape[1:]
    from_front = (lax.axis_index("depth") < lax.axis_size("depth") // 2) == lower_half

    def band(r, carry):
        here = pl.ds(pl.multiple_of(r * SUBLANES, SUBLANES), SUBLANES)
        for x in range(width // LANES):
            at = pl.ds(x * LANES, LANES)
            log_own, log_passed = own[2, here, at], passed[2, here, at]
            passing = jnp.exp2(jnp.where(from_front, log_passed, log_own))
            for channel in range(2):
                a, b = own[channel, here, at], passed[channel, here, at]
                front, back = jnp.where(from_front, b, a), jnp.where(from_front, a, b)
                out[channel, here, at] = front + passing * back
            out[2, here, at] = log_own + log_passed
        return carry

    lax.fori_loop(0, rows // SUBLANES, band, 0)


def fold(own, passed, lower_half=True):
    return pl.pallas_call(
        functools.partial(fold_kernel, lower_half),
        in_specs=[VMEM, VMEM],
        out_specs=VMEM,
        out_shape=jax.ShapeDtypeStruct(own.shape, jnp.float32),
        compiler_params=pltpu.CompilerParams(vmem_limit_bytes=16 << 20),
        name="fold",
    )(own, passed)


def send(part, pairs):
    return lax.ppermute(part, "depth", pairs)


def on_device(volume, transfer):
    slices, rows, columns = volume.shape
    groups = lax.axis_size("depth")
    total_slices = slices * groups
    width = columns // groups
    first, last, top, bottom = cut(volume)
    edges = (
        pass_on(last, "depth", True),
        pass_on(first, "depth", False),
        pass_on(bottom, "row", True),
        pass_on(top, "row", False),
    )
    half = slices // 2
    halves = [(0, half + 1, 0, rows), (half + 1, slices - half - 1, 0, rows)]
    ring = [
        (0, slices, 0, SUBLANES),
        (2, slices - 4, SUBLANES, 1),
        (2, slices - 4, rows - SUBLANES - 1, 1),
        (0, slices, rows - SUBLANES, SUBLANES),
        (0, 2, SUBLANES, rows - 2 * SUBLANES),
        (slices - 2, 2, SUBLANES, rows - 2 * SUBLANES),
    ]

    def stage(index, flip):
        if index:
            kernel = functools.partial(full_kernel, flip, 8, halves, total_slices)
            return render(kernel, halves, transfer, volume, edges, width, True)
        kernel = functools.partial(inner_kernel, flip, halves, total_slices)
        inner = render(kernel, halves, transfer, volume, (), width, False)
        kernel = functools.partial(rest_kernel, flip, ring, total_slices)
        return render(kernel, ring, transfer, volume, edges + (inner,), width, True)

    if groups == 4:
        inward, middle = [(0, 1), (3, 2)], [(1, 2), (2, 1)]
        far = stage(0, 3)
        passed = send(far, inward)
        second = fold(stage(1, 2), passed)
        from_outer = send(second, inward)
        from_inner = send(second, middle)
        third = fold(stage(2, 1), from_inner, False)
        beside = send(third, [(i, i ^ 1) for i in range(groups)])
        across = send(fold(far, from_outer), middle)
        return merge([across, beside, stage(3, 0)], [3, 1, 0], transfer)
    parts = []
    flips = list(range(groups - 1, -1, -1))
    for index, flip in enumerate(flips):
        part = stage(index, flip)
        if flip:
            part = send(part, [(i, i ^ flip) for i in range(groups)])
        parts.append(part)
    return merge(parts, flips, transfer)


def solution(mesh):
    in_specs = (P("depth", "row", None), P())
    out_specs = P(None, "row", "depth")

    return jax.shard_map(
        on_device, mesh=mesh, in_specs=in_specs, out_specs=out_specs, check_vma=False
    )
```

```python
import functools
import math

import jax
import jax.numpy as jnp
from jax import lax
from jax.experimental import pallas as pl
from jax.experimental.pallas import tpu as pltpu
from jax.sharding import PartitionSpec as P


LANES = 128
SUBLANES = 8
LN2 = math.log(2.0)
SMEM = pl.BlockSpec(memory_space=pltpu.SMEM)
VMEM = pl.BlockSpec(memory_space=pltpu.VMEM)
ANY = pl.BlockSpec(memory_space=pl.ANY)


def by_parity(axis, even, odd):
    is_even = lax.rem(lax.axis_index(axis), 2) == 0
    pl.when(is_even)(even)
    pl.when(jnp.logical_not(is_even))(odd)


def start(*copies):
    for copy in copies:
        copy.start()


def cut_kernel(volume, slab_a, slab_b, strip_a, strip_b, sems):
    slices, rows, _ = volume.shape

    def slab(z, i):
        target = (slab_a, slab_b)[i]
        return pltpu.make_async_copy(volume.at[pl.ds(z, 1)], target, sems.at[i])

    def strip(y, i):
        target = (strip_a, strip_b)[i]
        return pltpu.make_async_copy(volume.at[:, pl.ds(y, 1), :], target, sems.at[2 + i])

    by_parity(
        "depth",
        lambda: start(slab(slices - 1, 0), slab(0, 1)),
        lambda: start(slab(0, 0), slab(slices - 1, 1)),
    )
    by_parity(
        "row",
        lambda: start(strip(rows - 1, 0), strip(0, 1)),
        lambda: start(strip(0, 0), strip(rows - 1, 1)),
    )
    for i in range(2):
        slab(0, i).wait()
        strip(0, i).wait()


def cut(volume):
    slices, rows, columns = volume.shape
    slab = jax.ShapeDtypeStruct((1, rows, columns), jnp.float32)
    strip = jax.ShapeDtypeStruct((slices, 1, columns), jnp.float32)
    return pl.pallas_call(
        cut_kernel,
        in_specs=[ANY],
        out_specs=[VMEM] * 4,
        out_shape=[slab, slab, strip, strip],
        scratch_shapes=[pltpu.SemaphoreType.DMA((4,))],
        name="cut",
    )(volume)


def swap(value, axis, first):
    pairs = []
    for i in range(first, lax.axis_size(axis) - 1, 2):
        pairs += [(i, i + 1), (i + 1, i)]
    return lax.ppermute(value, axis, pairs)


def tile_constants():
    lane = lax.broadcasted_iota(jnp.int32, (SUBLANES, LANES), 1)
    return lane == 0, lane == LANES - 1


def coefficients(transfer, slices):
    gamma = jnp.full((SUBLANES, LANES), transfer[6], jnp.float32) * (-2.0 / slices)
    ambient = 0.5 * jnp.full((SUBLANES, LANES), transfer[7], jnp.float32)
    return gamma, (1.0 - ambient) / (3.0 * ambient)


def cell(cells, c, z, row, x, below, above, state, coef, ends):
    log_t, passing, shade, tinted = state
    gamma, ratio = coef
    first, last = ends
    here = pl.ds(row, SUBLANES)
    right = cells[c + 1, z, here, :]
    left = cells[c - 1, z, here, :]
    d_row = cells[c, z, pl.ds(row + 1, SUBLANES), :] - cells[c, z, pl.ds(row - 1, SUBLANES), :]
    to_right = pltpu.roll(jnp.where(first, right, x), LANES - 1, 1)
    to_left = pltpu.roll(jnp.where(last, left, x), 1, 1)
    d_col = to_right - to_left
    d_depth = above - below
    plane = d_row + d_col
    along = d_depth + (plane + plane)
    norm = d_depth * d_depth + (d_row * d_row + (d_col * d_col + 4.0))
    lambert = jnp.abs(along) * lax.rsqrt(norm)
    log_t = log_t + gamma * jnp.log2(1.0 + jnp.exp(x))
    after = jnp.exp2(log_t)
    taken = passing - after
    lit = taken * lambert
    shade = shade + lit
    tinted = tinted + (taken + ratio * lit) * jnp.tanh(x)
    return log_t, after, shade, tinted


def fresh_state():
    zero = jnp.zeros((SUBLANES, LANES), jnp.float32)
    return zero, jnp.ones((SUBLANES, LANES), jnp.float32), zero, zero


def put(out, c, row, state):
    log_t, _, shade, tinted = state
    rows = pl.ds(row - SUBLANES, SUBLANES)
    lanes = pl.ds((c - 1) * LANES, LANES)
    if not isinstance(row, int):
        rows = pl.ds(pl.multiple_of(row - SUBLANES, SUBLANES), SUBLANES)
    if not isinstance(c, int):
        lanes = pl.ds(pl.multiple_of((c - 1) * LANES, LANES), LANES)
    for channel, value in enumerate((shade, tinted, log_t)):
        out[channel, rows, lanes] = value


class Bricks:
    def __init__(self, volume, cells, sems, shift, chunks, pieces):
        self.volume, self.cells, self.sems, self.pieces = volume, cells, sems, pieces
        self.chunks = chunks
        self.total = volume.shape[2] // LANES
        block = lax.rem(lax.axis_index("depth") + shift, lax.axis_size("depth"))
        self.base = block * chunks
        self.has_left = self.base > 0
        self.has_right = self.base + chunks < self.total

    def lanes(self, c):
        at = jnp.clip(self.base + (c - 1), 0, self.total - 1)
        return pl.ds(pl.multiple_of(at * LANES, LANES), LANES)

    def copy(self, c, k):
        z, depth, y, height = self.pieces[k]
        return pltpu.make_async_copy(
            self.volume.at[pl.ds(z, depth), pl.ds(y, height), self.lanes(c)],
            self.cells.at[c, pl.ds(z + 1, depth), pl.ds(y + SUBLANES, height), :],
            self.sems.at[c, k],
        )

    def clear(self, c):
        slices, rows, _ = self.volume.shape
        zero = jnp.zeros((SUBLANES, LANES), jnp.float32)

        def slice_of(z, carry):
            for r in range(rows // SUBLANES):
                self.cells[c, z + 1, pl.ds(SUBLANES * (r + 1), SUBLANES), :] = zero
            return carry

        lax.fori_loop(0, slices, slice_of, 0)

    def start(self, k, chunks):
        for c in chunks:
            if c == 0:
                pl.when(self.has_left)(lambda: self.copy(0, k).start())
            elif c == self.chunks + 1:
                pl.when(self.has_right)(lambda: self.copy(self.chunks + 1, k).start())
            else:
                self.copy(c, k).start()

    def start_all(self):
        for k in range(len(self.pieces)):
            self.start(k, (1, 0, 2))
        for c in range(3, self.chunks + 2):
            for k in range(len(self.pieces)):
                self.start(k, (c,))
        pl.when(jnp.logical_not(self.has_left))(lambda: self.clear(0))
        pl.when(jnp.logical_not(self.has_right))(lambda: self.clear(self.chunks + 1))

    def land(self, c, k):
        @pl.when(c == 1)
        def _():
            self.copy(1, k).wait()
            self.copy(2, k).wait()
            pl.when(self.has_left)(lambda: self.copy(0, k).wait())

        @pl.when(jnp.logical_and(c > 1, jnp.logical_or(c < self.chunks, self.has_right)))
        def _():
            self.copy(c + 1, k).wait()


class Edges:
    def __init__(self, bricks, sems, slab_a, slab_b, strip_a, strip_b):
        self.bricks, self.sems = bricks, sems
        self.slabs, self.strips = (slab_a, slab_b), (strip_a, strip_b)

    def slab(self, c, side, source):
        slices, rows, _ = self.bricks.volume.shape
        return pltpu.make_async_copy(
            self.slabs[source].at[0, :, self.bricks.lanes(c)],
            self.bricks.cells.at[c, side * (slices + 1), pl.ds(SUBLANES, rows), :],
            self.sems.at[c, side],
        )

    def strip(self, c, side, source):
        slices, rows, _ = self.bricks.volume.shape
        row = (SUBLANES - 1, SUBLANES + rows)[side]
        return pltpu.make_async_copy(
            self.strips[source].at[:, :, self.bricks.lanes(c)],
            self.bricks.cells.at[c, pl.ds(1, slices), pl.ds(row, 1), :],
            self.sems.at[c, 2 + side],
        )

    def start(self, chunks):
        for axis, copy in (("depth", self.slab), ("row", self.strip)):
            by_parity(
                axis,
                lambda: start(*[copy(c, side, 1 - side) for c in chunks for side in range(2)]),
                lambda: start(*[copy(c, side, side) for c in chunks for side in range(2)]),
            )

    def wait(self, c):
        for side in range(2):
            self.slab(c, side, 0).wait()
            self.strip(c, side, 0).wait()


def march(cells, c, rows, begin, step, trips, coef, ends, arrive):
    def at(z):
        return [cells[c, z, pl.ds(row, SUBLANES), :] for row in rows]

    def trip(k, carry):
        arrive(k)
        states, belows, centers = carry
        for i in range(step):
            z = begin + 1 + k * step + i
            aboves = at(z + 1)
            states = [
                cell(cells, c, z, *tile, coef, ends)
                for tile in zip(rows, centers, belows, aboves, states)
            ]
            belows, centers = centers, aboves
        return states, belows, centers

    carry = ([fresh_state()] * len(rows), at(begin), at(begin + 1))
    if trips == 1:
        return trip(0, carry)[0]
    return lax.fori_loop(0, trips, trip, carry)[0]


def full_kernel(shift, tiles, pieces, total_slices, transfer, volume, *refs):
    *halo, out, cells, sems, edge_sems = refs
    slices, rows, _ = volume.shape
    chunks = out.shape[2] // LANES
    trips = len(pieces)
    groups = rows // SUBLANES // tiles
    bricks = Bricks(volume, cells, sems, shift, chunks, pieces)
    edges = Edges(bricks, edge_sems, *halo)
    bricks.start_all()
    edges.start(range(1, chunks + 1))
    coef = coefficients(transfer, total_slices)
    ends = tile_constants()

    def group(index, carry):
        c = index // groups + 1
        row = pl.multiple_of((index % groups * tiles + 1) * SUBLANES, SUBLANES)
        fresh = index % groups == 0

        @pl.when(fresh)
        def _():
            edges.wait(c)
            bricks.land(c, 0)

        def arrive(k):
            for part in range(1, trips):
                pl.when(jnp.logical_and(fresh, k == part))(lambda part=part: bricks.land(c, part))

        at_rows = [row + SUBLANES * t for t in range(tiles)]
        states = march(cells, c, at_rows, 0, slices // trips, trips, coef, ends, arrive)
        for at_row, state in zip(at_rows, states):
            put(out, c, at_row, state)
        return carry

    lax.fori_loop(0, chunks * groups, group, 0)


def inner_kernel(shift, pieces, total_slices, transfer, volume, out, cells, sems):
    slices, rows, _ = volume.shape
    chunks = out.shape[2] // LANES
    trips = len(pieces)
    bricks = Bricks(volume, cells, sems, shift, chunks, pieces)
    bricks.start_all()
    coef = coefficients(transfer, total_slices)
    ends = tile_constants()
    at_rows = [SUBLANES * (t + 2) for t in range(rows // SUBLANES - 2)]

    def group(index, carry):
        c = index + 1
        bricks.land(c, 0)

        def arrive(k):
            for part in range(1, trips):
                pl.when(k == part)(lambda part=part: bricks.land(c, part))

        states = march(
            cells, c, at_rows, 1, (slices - 2) // trips, trips, coef, ends, arrive
        )
        for at_row, state in zip(at_rows, states):
            put(out, c, at_row, state)
        return carry

    lax.fori_loop(0, chunks, group, 0)


def rest_kernel(shift, pieces, total_slices, transfer, volume, *refs):
    *halo, inner, out, cells, sems, edge_sems = refs
    slices, rows, _ = volume.shape
    chunks = out.shape[2] // LANES
    bricks = Bricks(volume, cells, sems, shift, chunks, pieces)
    edges = Edges(bricks, edge_sems, *halo)
    bricks.start_all()
    edges.start(range(1, chunks + 1))
    coef = coefficients(transfer, total_slices)
    ends = tile_constants()

    def group(index, carry):
        c = index + 1
        edges.wait(c)
        for k in range(len(pieces)):
            bricks.land(c, k)
        outer = [SUBLANES, rows]
        states = march(cells, c, outer, 0, slices, 1, coef, ends, lambda k: None)
        for at_row, state in zip(outer, states):
            put(out, c, at_row, state)
        lanes = pl.ds(pl.multiple_of((c - 1) * LANES, LANES), LANES)
        for t in range(1, rows // SUBLANES - 1):
            row = SUBLANES * (t + 1)
            here = pl.ds(row, SUBLANES)
            sides = []
            for z in (1, slices):
                below, x, above = [cells[c, z + i, here, :] for i in (-1, 0, 1)]
                sides.append(cell(cells, c, z, row, x, below, above, fresh_state(), coef, ends))
            (log_a, pass_a, shade_a, tint_a), (log_b, _, shade_b, tint_b) = sides
            shade, tint, log_t = [inner[i, pl.ds(row - SUBLANES, SUBLANES), lanes] for i in range(3)]
            passing = jnp.exp2(log_t)
            shade = shade_a + pass_a * (shade + passing * shade_b)
            tint = tint_a + pass_a * (tint + passing * tint_b)
            put(out, c, row, (log_a + log_t + log_b, None, shade, tint))
        return carry

    lax.fori_loop(0, chunks, group, 0)


def render(kernel, pieces, transfer, volume, extra, width, halo):
    slices, rows, _ = volume.shape
    chunks = width // LANES
    scratch = [
        pltpu.VMEM((chunks + 2, slices + 2, rows + 2 * SUBLANES, LANES), jnp.float32),
        pltpu.SemaphoreType.DMA((chunks + 2, len(pieces))),
    ]
    if halo:
        scratch.append(pltpu.SemaphoreType.DMA((chunks + 1, 4)))
    return pl.pallas_call(
        kernel,
        in_specs=[SMEM, ANY] + [ANY] * min(4, len(extra)) + [VMEM] * (len(extra) - 4),
        out_specs=VMEM,
        out_shape=jax.ShapeDtypeStruct((3, rows, width), jnp.float32),
        scratch_shapes=scratch,
        compiler_params=pltpu.CompilerParams(vmem_limit_bytes=32 << 20),
    )(transfer, volume, *extra)


def merge_kernel(shifts, transfer, *refs):
    *parts, out = refs
    count = len(parts)
    mine = lax.axis_index("depth")
    rows, width = out.shape[1:]
    sources = [lax.rem(mine - shift + count, count) for shift in shifts]
    nearer = [
        [jnp.where(sources[j] < sources[i], 1.0, 0.0) for j in range(count)] for i in range(count)
    ]
    ambient = 0.5 * jnp.full((SUBLANES, LANES), transfer[7], jnp.float32)
    spread = (1.0 - ambient) / 3.0

    def band(r, carry):
        here = pl.ds(pl.multiple_of(r * SUBLANES, SUBLANES), SUBLANES)
        for x in range(width // LANES):
            at = pl.ds(x * LANES, LANES)
            shade = tinted = log_t = jnp.zeros((SUBLANES, LANES), jnp.float32)
            logs = [part[2, here, at] for part in parts]
            for i, part in enumerate(parts):
                ahead = sum(logs[j] * nearer[i][j] for j in range(count) if j != i)
                passing = jnp.exp2(ahead)
                shade = shade + passing * part[0, here, at]
                tinted = tinted + passing * part[1, here, at]
                log_t = log_t + logs[i]
            half = jnp.tanh(log_t * (-0.5 * LN2))
            opacity = (half + half) / (1.0 + half)
            full = ambient * opacity + spread * shade
            mixed = 0.5 * (full + ambient * tinted)
            for color in range(3):
                out[color, here, at] = transfer[color] * full + transfer[3 + color] * mixed
            out[3, here, at] = opacity
        return carry

    lax.fori_loop(0, rows // SUBLANES, band, 0)


def merge(parts, shifts, transfer):
    _, rows, width = parts[0].shape
    return pl.pallas_call(
        functools.partial(merge_kernel, shifts),
        in_specs=[SMEM] + [VMEM] * len(parts),
        out_specs=VMEM,
        out_shape=jax.ShapeDtypeStruct((4, rows, width), jnp.float32),
        compiler_params=pltpu.CompilerParams(vmem_limit_bytes=16 << 20),
        name="merge",
    )(transfer, *parts)


def on_device(volume, transfer):
    slices, rows, columns = volume.shape
    groups = lax.axis_size("depth")
    total_slices = slices * groups
    width = columns // groups
    slab_a, slab_b, strip_a, strip_b = cut(volume)
    edges = (
        swap(slab_a, "depth", 0),
        swap(slab_b, "depth", 1),
        swap(strip_a, "row", 0),
        swap(strip_b, "row", 1),
    )
    half = slices // 2
    halves = [(0, half + 1, 0, rows), (half + 1, slices - half - 1, 0, rows)]
    ring = [
        (0, slices, 0, 2 * SUBLANES),
        (0, slices, rows - 2 * SUBLANES, 2 * SUBLANES),
        (0, 2, 2 * SUBLANES, rows - 4 * SUBLANES),
        (slices - 2, 2, 2 * SUBLANES, rows - 4 * SUBLANES),
    ]
    shifts = order_of_shifts(groups)
    parts = []
    for stage, shift in enumerate(shifts):
        if stage == 0:
            kernel = functools.partial(inner_kernel, shift, halves, total_slices)
            inner = render(kernel, halves, transfer, volume, (), width, False)
            kernel = functools.partial(rest_kernel, shift, ring, total_slices)
            part = render(kernel, ring, transfer, volume, edges + (inner,), width, True)
        else:
            kernel = functools.partial(full_kernel, shift, 8, halves, total_slices)
            part = render(kernel, halves, transfer, volume, edges, width, True)
        if shift:
            pairs = [(i, (i + shift) % groups) for i in range(groups)]
            part = lax.ppermute(part, "depth", pairs)
        parts.append(part)
    return merge(parts, shifts, transfer)


def order_of_shifts(groups):
    return sorted(range(1, groups), key=lambda s: -min(s, groups - s)) + [0]


def solution(mesh):
    in_specs = (P("depth", "row", None), P())
    out_specs = P(None, "row", "depth")

    return jax.shard_map(
        on_device, mesh=mesh, in_specs=in_specs, out_specs=out_specs, check_vma=False
    )
```

```python
import functools
import math

import jax
import jax.numpy as jnp
from jax import lax
from jax.experimental import pallas as pl
from jax.experimental.pallas import tpu as pltpu
from jax.sharding import PartitionSpec as P


LANES = 128
SUBLANES = 8
LN2 = math.log(2.0)
SMEM = pl.BlockSpec(memory_space=pltpu.SMEM)
VMEM = pl.BlockSpec(memory_space=pltpu.VMEM)
ANY = pl.BlockSpec(memory_space=pl.ANY)


def by_parity(axis, even, odd):
    is_even = lax.rem(lax.axis_index(axis), 2) == 0
    pl.when(is_even)(even)
    pl.when(jnp.logical_not(is_even))(odd)


def start(*copies):
    for copy in copies:
        copy.start()


def cut_kernel(volume, slab_a, slab_b, strip_a, strip_b, sems):
    slices, rows, _ = volume.shape

    def slab(z, i):
        target = (slab_a, slab_b)[i]
        return pltpu.make_async_copy(volume.at[pl.ds(z, 1)], target, sems.at[i])

    def strip(y, i):
        target = (strip_a, strip_b)[i]
        return pltpu.make_async_copy(volume.at[:, pl.ds(y, 1), :], target, sems.at[2 + i])

    by_parity(
        "depth",
        lambda: start(slab(slices - 1, 0), slab(0, 1)),
        lambda: start(slab(0, 0), slab(slices - 1, 1)),
    )
    by_parity(
        "row",
        lambda: start(strip(rows - 1, 0), strip(0, 1)),
        lambda: start(strip(0, 0), strip(rows - 1, 1)),
    )
    for i in range(2):
        slab(0, i).wait()
        strip(0, i).wait()


def cut(volume):
    slices, rows, columns = volume.shape
    slab = jax.ShapeDtypeStruct((1, rows, columns), jnp.float32)
    strip = jax.ShapeDtypeStruct((slices, 1, columns), jnp.float32)
    return pl.pallas_call(
        cut_kernel,
        in_specs=[ANY],
        out_specs=[VMEM] * 4,
        out_shape=[slab, slab, strip, strip],
        scratch_shapes=[pltpu.SemaphoreType.DMA((4,))],
        name="cut",
    )(volume)


def swap(value, axis, first):
    pairs = []
    for i in range(first, lax.axis_size(axis) - 1, 2):
        pairs += [(i, i + 1), (i + 1, i)]
    return lax.ppermute(value, axis, pairs)


def tile_constants():
    lane = lax.broadcasted_iota(jnp.int32, (SUBLANES, LANES), 1)
    return lane == 0, lane == LANES - 1


def coefficients(transfer, slices):
    gamma = jnp.full((SUBLANES, LANES), transfer[6], jnp.float32) * (-2.0 / slices)
    ambient = 0.5 * jnp.full((SUBLANES, LANES), transfer[7], jnp.float32)
    return gamma, (1.0 - ambient) / (3.0 * ambient)


def cell(cells, c, z, row, x, below, above, state, coef, ends):
    log_t, passing, shade, tinted = state
    gamma, ratio = coef
    first, last = ends
    here = pl.ds(row, SUBLANES)
    right = cells[c + 1, z, here, :]
    left = cells[c - 1, z, here, :]
    d_row = cells[c, z, pl.ds(row + 1, SUBLANES), :] - cells[c, z, pl.ds(row - 1, SUBLANES), :]
    to_right = pltpu.roll(jnp.where(first, right, x), LANES - 1, 1)
    to_left = pltpu.roll(jnp.where(last, left, x), 1, 1)
    d_col = to_right - to_left
    d_depth = above - below
    plane = d_row + d_col
    along = d_depth + (plane + plane)
    norm = d_depth * d_depth + (d_row * d_row + (d_col * d_col + 4.0))
    lambert = jnp.abs(along) * lax.rsqrt(norm)
    log_t = log_t + gamma * jnp.log2(1.0 + jnp.exp(x))
    after = jnp.exp2(log_t)
    taken = passing - after
    lit = taken * lambert
    shade = shade + lit
    tinted = tinted + (taken + ratio * lit) * jnp.tanh(x)
    return log_t, after, shade, tinted


def fresh_state():
    zero = jnp.zeros((SUBLANES, LANES), jnp.float32)
    return zero, jnp.ones((SUBLANES, LANES), jnp.float32), zero, zero


def put(out, c, row, state):
    log_t, _, shade, tinted = state
    rows = pl.ds(row - SUBLANES, SUBLANES)
    lanes = pl.ds((c - 1) * LANES, LANES)
    if not isinstance(row, int):
        rows = pl.ds(pl.multiple_of(row - SUBLANES, SUBLANES), SUBLANES)
    if not isinstance(c, int):
        lanes = pl.ds(pl.multiple_of((c - 1) * LANES, LANES), LANES)
    for channel, value in enumerate((shade, tinted, log_t)):
        out[channel, rows, lanes] = value


class Bricks:
    def __init__(self, volume, cells, sems, shift, chunks, pieces):
        self.volume, self.cells, self.sems, self.pieces = volume, cells, sems, pieces
        self.chunks = chunks
        self.total = volume.shape[2] // LANES
        block = lax.rem(lax.axis_index("depth") + shift, lax.axis_size("depth"))
        self.base = block * chunks
        self.has_left = self.base > 0
        self.has_right = self.base + chunks < self.total

    def lanes(self, c):
        at = jnp.clip(self.base + (c - 1), 0, self.total - 1)
        return pl.ds(pl.multiple_of(at * LANES, LANES), LANES)

    def copy(self, c, k):
        z, depth, y, height = self.pieces[k]
        return pltpu.make_async_copy(
            self.volume.at[pl.ds(z, depth), pl.ds(y, height), self.lanes(c)],
            self.cells.at[c, pl.ds(z + 1, depth), pl.ds(y + SUBLANES, height), :],
            self.sems.at[c, k],
        )

    def clear(self, c):
        slices, rows, _ = self.volume.shape
        zero = jnp.zeros((SUBLANES, LANES), jnp.float32)

        def slice_of(z, carry):
            for r in range(rows // SUBLANES):
                self.cells[c, z + 1, pl.ds(SUBLANES * (r + 1), SUBLANES), :] = zero
            return carry

        lax.fori_loop(0, slices, slice_of, 0)

    def start(self, k, chunks):
        for c in chunks:
            if c == 0:
                pl.when(self.has_left)(lambda: self.copy(0, k).start())
            elif c == self.chunks + 1:
                pl.when(self.has_right)(lambda: self.copy(self.chunks + 1, k).start())
            else:
                self.copy(c, k).start()

    def start_all(self):
        for k in range(len(self.pieces)):
            self.start(k, (1, 0, 2))
        for c in range(3, self.chunks + 2):
            for k in range(len(self.pieces)):
                self.start(k, (c,))
        pl.when(jnp.logical_not(self.has_left))(lambda: self.clear(0))
        pl.when(jnp.logical_not(self.has_right))(lambda: self.clear(self.chunks + 1))

    def land(self, c, k):
        @pl.when(c == 1)
        def _():
            self.copy(1, k).wait()
            self.copy(2, k).wait()
            pl.when(self.has_left)(lambda: self.copy(0, k).wait())

        @pl.when(jnp.logical_and(c > 1, jnp.logical_or(c < self.chunks, self.has_right)))
        def _():
            self.copy(c + 1, k).wait()


class Edges:
    def __init__(self, bricks, sems, slab_a, slab_b, strip_a, strip_b):
        self.bricks, self.sems = bricks, sems
        self.slabs, self.strips = (slab_a, slab_b), (strip_a, strip_b)

    def slab(self, c, side, source):
        slices, rows, _ = self.bricks.volume.shape
        return pltpu.make_async_copy(
            self.slabs[source].at[0, :, self.bricks.lanes(c)],
            self.bricks.cells.at[c, side * (slices + 1), pl.ds(SUBLANES, rows), :],
            self.sems.at[c, side],
        )

    def strip(self, c, side, source):
        slices, rows, _ = self.bricks.volume.shape
        row = (SUBLANES - 1, SUBLANES + rows)[side]
        return pltpu.make_async_copy(
            self.strips[source].at[:, :, self.bricks.lanes(c)],
            self.bricks.cells.at[c, pl.ds(1, slices), pl.ds(row, 1), :],
            self.sems.at[c, 2 + side],
        )

    def start(self, chunks):
        for axis, copy in (("depth", self.slab), ("row", self.strip)):
            by_parity(
                axis,
                lambda: start(*[copy(c, side, 1 - side) for c in chunks for side in range(2)]),
                lambda: start(*[copy(c, side, side) for c in chunks for side in range(2)]),
            )

    def wait(self, c):
        for side in range(2):
            self.slab(c, side, 0).wait()
            self.strip(c, side, 0).wait()


def march(cells, c, rows, begin, step, trips, coef, ends, arrive):
    def at(z):
        return [cells[c, z, pl.ds(row, SUBLANES), :] for row in rows]

    def trip(k, carry):
        arrive(k)
        states, belows, centers = carry
        for i in range(step):
            z = begin + 1 + k * step + i
            aboves = at(z + 1)
            states = [
                cell(cells, c, z, *tile, coef, ends)
                for tile in zip(rows, centers, belows, aboves, states)
            ]
            belows, centers = centers, aboves
        return states, belows, centers

    carry = ([fresh_state()] * len(rows), at(begin), at(begin + 1))
    if trips == 1:
        return trip(0, carry)[0]
    return lax.fori_loop(0, trips, trip, carry)[0]


def full_kernel(shift, tiles, pieces, total_slices, transfer, volume, *refs):
    *halo, out, cells, sems, edge_sems = refs
    slices, rows, _ = volume.shape
    chunks = out.shape[2] // LANES
    trips = len(pieces)
    groups = rows // SUBLANES // tiles
    bricks = Bricks(volume, cells, sems, shift, chunks, pieces)
    edges = Edges(bricks, edge_sems, *halo)
    bricks.start_all()
    edges.start(range(1, chunks + 1))
    coef = coefficients(transfer, total_slices)
    ends = tile_constants()

    def group(index, carry):
        c = index // groups + 1
        row = pl.multiple_of((index % groups * tiles + 1) * SUBLANES, SUBLANES)
        fresh = index % groups == 0

        @pl.when(fresh)
        def _():
            edges.wait(c)
            bricks.land(c, 0)

        def arrive(k):
            for part in range(1, trips):
                pl.when(jnp.logical_and(fresh, k == part))(lambda part=part: bricks.land(c, part))

        at_rows = [row + SUBLANES * t for t in range(tiles)]
        states = march(cells, c, at_rows, 0, slices // trips, trips, coef, ends, arrive)
        for at_row, state in zip(at_rows, states):
            put(out, c, at_row, state)
        return carry

    lax.fori_loop(0, chunks * groups, group, 0)


def inner_kernel(shift, pieces, total_slices, transfer, volume, out, cells, sems):
    slices, rows, _ = volume.shape
    chunks = out.shape[2] // LANES
    trips = len(pieces)
    bricks = Bricks(volume, cells, sems, shift, chunks, pieces)
    bricks.start_all()
    coef = coefficients(transfer, total_slices)
    ends = tile_constants()
    at_rows = [SUBLANES * (t + 2) for t in range(rows // SUBLANES - 2)]

    def group(index, carry):
        c = index + 1
        bricks.land(c, 0)

        def arrive(k):
            for part in range(1, trips):
                pl.when(k == part)(lambda part=part: bricks.land(c, part))

        states = march(
            cells, c, at_rows, 1, (slices - 2) // trips, trips, coef, ends, arrive
        )
        for at_row, state in zip(at_rows, states):
            put(out, c, at_row, state)
        return carry

    lax.fori_loop(0, chunks, group, 0)


def rest_kernel(shift, total_slices, transfer, volume, *refs):
    *halo, inner, _, out, cells, edge_sems = refs
    slices, rows, _ = volume.shape
    chunks = out.shape[2] // LANES
    bricks = Bricks(volume, cells, None, shift, chunks, ())
    edges = Edges(bricks, edge_sems, *halo)
    edges.start(range(1, chunks + 1))
    coef = coefficients(transfer, total_slices)
    ends = tile_constants()

    def group(index, carry):
        c = index + 1
        edges.wait(c)
        outer = [SUBLANES, rows]
        states = march(cells, c, outer, 0, slices, 1, coef, ends, lambda k: None)
        for at_row, state in zip(outer, states):
            put(out, c, at_row, state)
        lanes = pl.ds(pl.multiple_of((c - 1) * LANES, LANES), LANES)
        for t in range(1, rows // SUBLANES - 1):
            row = SUBLANES * (t + 1)
            here = pl.ds(row, SUBLANES)
            sides = []
            for z in (1, slices):
                below, x, above = [cells[c, z + i, here, :] for i in (-1, 0, 1)]
                sides.append(cell(cells, c, z, row, x, below, above, fresh_state(), coef, ends))
            (log_a, pass_a, shade_a, tint_a), (log_b, _, shade_b, tint_b) = sides
            shade, tint, log_t = [inner[i, pl.ds(row - SUBLANES, SUBLANES), lanes] for i in range(3)]
            passing = jnp.exp2(log_t)
            shade = shade_a + pass_a * (shade + passing * shade_b)
            tint = tint_a + pass_a * (tint + passing * tint_b)
            put(out, c, row, (log_a + log_t + log_b, None, shade, tint))
        return carry

    lax.fori_loop(0, chunks, group, 0)


def cells_shape(volume, width):
    slices, rows, _ = volume.shape
    return (width // LANES + 2, slices + 2, rows + 2 * SUBLANES, LANES)


def render_inner(kernel, pieces, transfer, volume, width):
    shape = cells_shape(volume, width)
    return pl.pallas_call(
        kernel,
        in_specs=[SMEM, ANY],
        out_specs=[VMEM] * 2,
        out_shape=[
            jax.ShapeDtypeStruct((3, volume.shape[1], width), jnp.float32),
            jax.ShapeDtypeStruct(shape, jnp.float32),
        ],
        scratch_shapes=[pltpu.SemaphoreType.DMA((shape[0], len(pieces)))],
        compiler_params=pltpu.CompilerParams(vmem_limit_bytes=32 << 20),
        name="inner",
    )(transfer, volume)


def render_rest(kernel, transfer, volume, halo, inner, cells):
    out = jax.ShapeDtypeStruct(inner.shape, jnp.float32)
    return pl.pallas_call(
        kernel,
        in_specs=[SMEM, ANY] + [ANY] * 4 + [VMEM] * 2,
        out_specs=[VMEM] * 2,
        out_shape=[out, jax.ShapeDtypeStruct(cells.shape, jnp.float32)],
        input_output_aliases={7: 1},
        scratch_shapes=[pltpu.SemaphoreType.DMA((cells.shape[0] - 1, 4))],
        compiler_params=pltpu.CompilerParams(vmem_limit_bytes=32 << 20),
        name="rest",
    )(transfer, volume, *halo, inner, cells)[0]


def render(kernel, pieces, transfer, volume, extra, width, halo):
    slices, rows, _ = volume.shape
    chunks = width // LANES
    scratch = [
        pltpu.VMEM((chunks + 2, slices + 2, rows + 2 * SUBLANES, LANES), jnp.float32),
        pltpu.SemaphoreType.DMA((chunks + 2, len(pieces))),
    ]
    if halo:
        scratch.append(pltpu.SemaphoreType.DMA((chunks + 1, 4)))
    return pl.pallas_call(
        kernel,
        in_specs=[SMEM, ANY] + [ANY] * min(4, len(extra)) + [VMEM] * (len(extra) - 4),
        out_specs=VMEM,
        out_shape=jax.ShapeDtypeStruct((3, rows, width), jnp.float32),
        scratch_shapes=scratch,
        compiler_params=pltpu.CompilerParams(vmem_limit_bytes=32 << 20),
    )(transfer, volume, *extra)


def merge_kernel(shifts, transfer, *refs):
    *parts, out = refs
    count = len(parts)
    mine = lax.axis_index("depth")
    rows, width = out.shape[1:]
    sources = [lax.rem(mine - shift + count, count) for shift in shifts]
    nearer = [
        [jnp.where(sources[j] < sources[i], 1.0, 0.0) for j in range(count)] for i in range(count)
    ]
    ambient = 0.5 * jnp.full((SUBLANES, LANES), transfer[7], jnp.float32)
    spread = (1.0 - ambient) / 3.0

    def band(r, carry):
        here = pl.ds(pl.multiple_of(r * SUBLANES, SUBLANES), SUBLANES)
        for x in range(width // LANES):
            at = pl.ds(x * LANES, LANES)
            shade = tinted = log_t = jnp.zeros((SUBLANES, LANES), jnp.float32)
            logs = [part[2, here, at] for part in parts]
            for i, part in enumerate(parts):
                ahead = sum(logs[j] * nearer[i][j] for j in range(count) if j != i)
                passing = jnp.exp2(ahead)
                shade = shade + passing * part[0, here, at]
                tinted = tinted + passing * part[1, here, at]
                log_t = log_t + logs[i]
            half = jnp.tanh(log_t * (-0.5 * LN2))
            opacity = (half + half) / (1.0 + half)
            full = ambient * opacity + spread * shade
            mixed = 0.5 * (full + ambient * tinted)
            for color in range(3):
                out[color, here, at] = transfer[color] * full + transfer[3 + color] * mixed
            out[3, here, at] = opacity
        return carry

    lax.fori_loop(0, rows // SUBLANES, band, 0)


def merge(parts, shifts, transfer):
    _, rows, width = parts[0].shape
    return pl.pallas_call(
        functools.partial(merge_kernel, shifts),
        in_specs=[SMEM] + [VMEM] * len(parts),
        out_specs=VMEM,
        out_shape=jax.ShapeDtypeStruct((4, rows, width), jnp.float32),
        compiler_params=pltpu.CompilerParams(vmem_limit_bytes=16 << 20),
        name="merge",
    )(transfer, *parts)


def on_device(volume, transfer):
    slices, rows, columns = volume.shape
    groups = lax.axis_size("depth")
    total_slices = slices * groups
    width = columns // groups
    slab_a, slab_b, strip_a, strip_b = cut(volume)
    edges = (
        swap(slab_a, "depth", 0),
        swap(slab_b, "depth", 1),
        swap(strip_a, "row", 0),
        swap(strip_b, "row", 1),
    )
    half = slices // 2
    halves = [(0, half + 1, 0, rows), (half + 1, slices - half - 1, 0, rows)]
    shifts = order_of_shifts(groups)
    parts = []
    for stage, shift in enumerate(shifts):
        if stage == 0:
            kernel = functools.partial(inner_kernel, shift, halves, total_slices)
            inner, cells = render_inner(kernel, halves, transfer, volume, width)
            kernel = functools.partial(rest_kernel, shift, total_slices)
            part = render_rest(kernel, transfer, volume, edges, inner, cells)
        else:
            kernel = functools.partial(full_kernel, shift, 8, halves, total_slices)
            part = render(kernel, halves, transfer, volume, edges, width, True)
        if shift:
            pairs = [(i, (i + shift) % groups) for i in range(groups)]
            part = lax.ppermute(part, "depth", pairs)
        parts.append(part)
    return merge(parts, shifts, transfer)


def order_of_shifts(groups):
    return sorted(range(1, groups), key=lambda s: -min(s, groups - s)) + [0]


def solution(mesh):
    in_specs = (P("depth", "row", None), P())
    out_specs = P(None, "row", "depth")

    return jax.shard_map(
        on_device, mesh=mesh, in_specs=in_specs, out_specs=out_specs, check_vma=False
    )
```

```python
import functools
import math

import jax
import jax.numpy as jnp
from jax import lax
from jax.experimental import pallas as pl
from jax.experimental.pallas import tpu as pltpu
from jax.sharding import PartitionSpec as P


LANES = 128
SUBLANES = 8
LN2 = math.log(2.0)
SMEM = pl.BlockSpec(memory_space=pltpu.SMEM)
VMEM = pl.BlockSpec(memory_space=pltpu.VMEM)
ANY = pl.BlockSpec(memory_space=pl.ANY)


def by_parity(axis, even, odd):
    is_even = lax.rem(lax.axis_index(axis), 2) == 0
    pl.when(is_even)(even)
    pl.when(jnp.logical_not(is_even))(odd)


def start(*copies):
    for copy in copies:
        copy.start()


def cut_kernel(volume, slab_a, slab_b, strip_a, strip_b, sems):
    slices, rows, _ = volume.shape

    def slab(z, i):
        target = (slab_a, slab_b)[i]
        return pltpu.make_async_copy(volume.at[pl.ds(z, 1)], target, sems.at[i])

    def strip(y, i):
        target = (strip_a, strip_b)[i]
        return pltpu.make_async_copy(volume.at[:, pl.ds(y, 1), :], target, sems.at[2 + i])

    by_parity(
        "depth",
        lambda: start(slab(slices - 1, 0), slab(0, 1)),
        lambda: start(slab(0, 0), slab(slices - 1, 1)),
    )
    by_parity(
        "row",
        lambda: start(strip(rows - 1, 0), strip(0, 1)),
        lambda: start(strip(0, 0), strip(rows - 1, 1)),
    )
    for i in range(2):
        slab(0, i).wait()
        strip(0, i).wait()


def cut(volume):
    slices, rows, columns = volume.shape
    slab = jax.ShapeDtypeStruct((1, rows, columns), jnp.float32)
    strip = jax.ShapeDtypeStruct((slices, 1, columns), jnp.float32)
    return pl.pallas_call(
        cut_kernel,
        in_specs=[ANY],
        out_specs=[VMEM] * 4,
        out_shape=[slab, slab, strip, strip],
        scratch_shapes=[pltpu.SemaphoreType.DMA((4,))],
        name="cut",
    )(volume)


def swap(value, axis, first):
    pairs = []
    for i in range(first, lax.axis_size(axis) - 1, 2):
        pairs += [(i, i + 1), (i + 1, i)]
    return lax.ppermute(value, axis, pairs)


def tile_constants():
    lane = lax.broadcasted_iota(jnp.int32, (SUBLANES, LANES), 1)
    return lane == 0, lane == LANES - 1


def coefficients(transfer, slices):
    gamma = jnp.full((SUBLANES, LANES), transfer[6], jnp.float32) * (-2.0 / slices)
    ambient = 0.5 * jnp.full((SUBLANES, LANES), transfer[7], jnp.float32)
    return gamma, (1.0 - ambient) / (3.0 * ambient)


def cell(cells, c, z, row, x, below, above, state, coef, ends):
    log_t, passing, shade, tinted = state
    gamma, ratio = coef
    first, last = ends
    here = pl.ds(row, SUBLANES)
    right = cells[c + 1, z, here, :]
    left = cells[c - 1, z, here, :]
    d_row = cells[c, z, pl.ds(row + 1, SUBLANES), :] - cells[c, z, pl.ds(row - 1, SUBLANES), :]
    to_right = pltpu.roll(jnp.where(first, right, x), LANES - 1, 1)
    to_left = pltpu.roll(jnp.where(last, left, x), 1, 1)
    d_col = to_right - to_left
    d_depth = above - below
    plane = d_row + d_col
    along = d_depth + (plane + plane)
    norm = d_depth * d_depth + (d_row * d_row + (d_col * d_col + 4.0))
    lambert = jnp.abs(along) * lax.rsqrt(norm)
    log_t = log_t + gamma * jnp.log2(1.0 + jnp.exp(x))
    after = jnp.exp2(log_t)
    taken = passing - after
    lit = taken * lambert
    shade = shade + lit
    tinted = tinted + (taken + ratio * lit) * jnp.tanh(x)
    return log_t, after, shade, tinted


def fresh_state():
    zero = jnp.zeros((SUBLANES, LANES), jnp.float32)
    return zero, jnp.ones((SUBLANES, LANES), jnp.float32), zero, zero


def put(out, c, row, state):
    log_t, _, shade, tinted = state
    rows = pl.ds(row - SUBLANES, SUBLANES)
    lanes = pl.ds((c - 1) * LANES, LANES)
    if not isinstance(row, int):
        rows = pl.ds(pl.multiple_of(row - SUBLANES, SUBLANES), SUBLANES)
    if not isinstance(c, int):
        lanes = pl.ds(pl.multiple_of((c - 1) * LANES, LANES), LANES)
    for channel, value in enumerate((shade, tinted, log_t)):
        out[channel, rows, lanes] = value


class Bricks:
    def __init__(self, volume, cells, sems, shift, chunks, pieces):
        self.volume, self.cells, self.sems, self.pieces = volume, cells, sems, pieces
        self.chunks = chunks
        self.total = volume.shape[2] // LANES
        block = lax.rem(lax.axis_index("depth") + shift, lax.axis_size("depth"))
        self.base = block * chunks
        self.has_left = self.base > 0
        self.has_right = self.base + chunks < self.total

    def lanes(self, c):
        at = jnp.clip(self.base + (c - 1), 0, self.total - 1)
        return pl.ds(pl.multiple_of(at * LANES, LANES), LANES)

    def copy(self, c, k):
        z, depth, y, height = self.pieces[k]
        return pltpu.make_async_copy(
            self.volume.at[pl.ds(z, depth), pl.ds(y, height), self.lanes(c)],
            self.cells.at[c, pl.ds(z + 1, depth), pl.ds(y + SUBLANES, height), :],
            self.sems.at[c, k],
        )

    def clear(self, c):
        slices, rows, _ = self.volume.shape
        zero = jnp.zeros((SUBLANES, LANES), jnp.float32)

        def slice_of(z, carry):
            for r in range(rows // SUBLANES):
                self.cells[c, z + 1, pl.ds(SUBLANES * (r + 1), SUBLANES), :] = zero
            return carry

        lax.fori_loop(0, slices, slice_of, 0)

    def start(self, k, chunks):
        for c in chunks:
            if c == 0:
                pl.when(self.has_left)(lambda: self.copy(0, k).start())
            elif c == self.chunks + 1:
                pl.when(self.has_right)(lambda: self.copy(self.chunks + 1, k).start())
            else:
                self.copy(c, k).start()

    def start_all(self):
        for k in range(len(self.pieces)):
            self.start(k, (1, 0, 2))
        for c in range(3, self.chunks + 2):
            for k in range(len(self.pieces)):
                self.start(k, (c,))
        pl.when(jnp.logical_not(self.has_left))(lambda: self.clear(0))
        pl.when(jnp.logical_not(self.has_right))(lambda: self.clear(self.chunks + 1))

    def land_all(self):
        for k in range(len(self.pieces)):
            for c in range(1, self.chunks + 1):
                self.copy(c, k).wait()
            pl.when(self.has_left)(lambda k=k: self.copy(0, k).wait())
            pl.when(self.has_right)(lambda k=k: self.copy(self.chunks + 1, k).wait())

    def land(self, c, k):
        @pl.when(c == 1)
        def _():
            self.copy(1, k).wait()
            self.copy(2, k).wait()
            pl.when(self.has_left)(lambda: self.copy(0, k).wait())

        @pl.when(jnp.logical_and(c > 1, jnp.logical_or(c < self.chunks, self.has_right)))
        def _():
            self.copy(c + 1, k).wait()


class Edges:
    def __init__(self, bricks, sems, slab_a, slab_b, strip_a, strip_b):
        self.bricks, self.sems = bricks, sems
        self.slabs, self.strips = (slab_a, slab_b), (strip_a, strip_b)

    def slab(self, c, side, source):
        slices, rows, _ = self.bricks.volume.shape
        return pltpu.make_async_copy(
            self.slabs[source].at[0, :, self.bricks.lanes(c)],
            self.bricks.cells.at[c, side * (slices + 1), pl.ds(SUBLANES, rows), :],
            self.sems.at[c, side],
        )

    def strip(self, c, side, source):
        slices, rows, _ = self.bricks.volume.shape
        row = (SUBLANES - 1, SUBLANES + rows)[side]
        return pltpu.make_async_copy(
            self.strips[source].at[:, :, self.bricks.lanes(c)],
            self.bricks.cells.at[c, pl.ds(1, slices), pl.ds(row, 1), :],
            self.sems.at[c, 2 + side],
        )

    def start(self, chunks):
        for axis, copy in (("depth", self.slab), ("row", self.strip)):
            by_parity(
                axis,
                lambda: start(*[copy(c, side, 1 - side) for c in chunks for side in range(2)]),
                lambda: start(*[copy(c, side, side) for c in chunks for side in range(2)]),
            )

    def wait(self, c):
        for side in range(2):
            self.slab(c, side, 0).wait()
            self.strip(c, side, 0).wait()


def march(cells, c, rows, begin, step, trips, coef, ends, arrive):
    def at(z):
        return [cells[c, z, pl.ds(row, SUBLANES), :] for row in rows]

    def trip(k, carry):
        arrive(k)
        states, belows, centers = carry
        for i in range(step):
            z = begin + 1 + k * step + i
            aboves = at(z + 1)
            states = [
                cell(cells, c, z, *tile, coef, ends)
                for tile in zip(rows, centers, belows, aboves, states)
            ]
            belows, centers = centers, aboves
        return states, belows, centers

    carry = ([fresh_state()] * len(rows), at(begin), at(begin + 1))
    if trips == 1:
        return trip(0, carry)[0]
    return lax.fori_loop(0, trips, trip, carry)[0]


def full_kernel(shift, later, step, pieces, total_slices, transfer, volume, *refs):
    slices, rows, _ = volume.shape
    halo, refs = refs[:4], refs[4:]
    if later is None:
        _, out, cells, edge_sems = refs
    else:
        _, _, out, cells, ahead, edge_sems, later_sems = refs
    chunks = out.shape[2] // LANES
    if later is not None:
        following = Bricks(volume, ahead, later_sems, later, chunks, pieces)
        following.start_all()
    bricks = Bricks(volume, cells, None, shift, chunks, ())
    edges = Edges(bricks, edge_sems, *halo)
    edges.start(range(1, chunks + 1))
    coef = coefficients(transfer, total_slices)
    ends = tile_constants()
    at_rows = [SUBLANES * (t + 1) for t in range(rows // SUBLANES)]

    def group(index, carry):
        c = index + 1
        edges.wait(c)
        states = march(cells, c, at_rows, 0, step, slices // step, coef, ends, lambda k: None)
        for at_row, state in zip(at_rows, states):
            put(out, c, at_row, state)
        return carry

    lax.fori_loop(0, chunks, group, 0)
    if later is not None:
        following.land_all()


def inner_kernel(shift, later, pieces, total_slices, transfer, volume, out, cells, ahead, sems, later_sems):
    slices, rows, _ = volume.shape
    chunks = out.shape[2] // LANES
    trips = len(pieces)
    bricks = Bricks(volume, cells, sems, shift, chunks, pieces)
    bricks.start_all()
    following = Bricks(volume, ahead, later_sems, later, chunks, pieces)
    following.start_all()
    coef = coefficients(transfer, total_slices)
    ends = tile_constants()
    at_rows = [SUBLANES * (t + 2) for t in range(rows // SUBLANES - 2)]

    def group(index, carry):
        c = index + 1
        bricks.land(c, 0)

        def arrive(k):
            for part in range(1, trips):
                pl.when(k == part)(lambda part=part: bricks.land(c, part))

        states = march(
            cells, c, at_rows, 1, (slices - 2) // trips, trips, coef, ends, arrive
        )
        for at_row, state in zip(at_rows, states):
            put(out, c, at_row, state)
        return carry

    lax.fori_loop(0, chunks, group, 0)
    following.land_all()


def rest_kernel(shift, total_slices, transfer, volume, *refs):
    *halo, inner, _, out, cells, edge_sems = refs
    slices, rows, _ = volume.shape
    chunks = out.shape[2] // LANES
    bricks = Bricks(volume, cells, None, shift, chunks, ())
    edges = Edges(bricks, edge_sems, *halo)
    edges.start(range(1, chunks + 1))
    coef = coefficients(transfer, total_slices)
    ends = tile_constants()

    def group(index, carry):
        c = index + 1
        edges.wait(c)
        outer = [SUBLANES, rows]
        states = march(cells, c, outer, 0, slices, 1, coef, ends, lambda k: None)
        for at_row, state in zip(outer, states):
            put(out, c, at_row, state)
        lanes = pl.ds(pl.multiple_of((c - 1) * LANES, LANES), LANES)
        for t in range(1, rows // SUBLANES - 1):
            row = SUBLANES * (t + 1)
            here = pl.ds(row, SUBLANES)
            sides = []
            for z in (1, slices):
                below, x, above = [cells[c, z + i, here, :] for i in (-1, 0, 1)]
                sides.append(cell(cells, c, z, row, x, below, above, fresh_state(), coef, ends))
            (log_a, pass_a, shade_a, tint_a), (log_b, _, shade_b, tint_b) = sides
            shade, tint, log_t = [inner[i, pl.ds(row - SUBLANES, SUBLANES), lanes] for i in range(3)]
            passing = jnp.exp2(log_t)
            shade = shade_a + pass_a * (shade + passing * shade_b)
            tint = tint_a + pass_a * (tint + passing * tint_b)
            put(out, c, row, (log_a + log_t + log_b, None, shade, tint))
        return carry

    lax.fori_loop(0, chunks, group, 0)


def cells_shape(volume, width):
    slices, rows, _ = volume.shape
    return (width // LANES + 2, slices + 2, rows + 2 * SUBLANES, LANES)


def call(kernel, transfer, volume, halo, done, buffers, fresh, counts, width, limit=16):
    shape = cells_shape(volume, width)
    held = jax.ShapeDtypeStruct(shape, jnp.float32)
    first = 2 + len(halo) + len(done)
    scratch = [pltpu.SemaphoreType.DMA((shape[0], count)) for count in counts]
    return pl.pallas_call(
        kernel,
        in_specs=[SMEM, ANY] + [ANY] * len(halo) + [VMEM] * (len(done) + len(buffers)),
        out_specs=[VMEM] * (1 + len(buffers) + fresh),
        out_shape=[jax.ShapeDtypeStruct((3, volume.shape[1], width), jnp.float32)]
        + [held] * (len(buffers) + fresh),
        input_output_aliases={first + i: 1 + i for i in range(len(buffers))},
        scratch_shapes=scratch,
        compiler_params=pltpu.CompilerParams(vmem_limit_bytes=limit << 20),
    )(transfer, volume, *halo, *done, *buffers)


def merge_kernel(shifts, transfer, *refs):
    *parts, out = refs
    count = len(parts)
    mine = lax.axis_index("depth")
    rows, width = out.shape[1:]
    sources = [lax.rem(mine - shift + count, count) for shift in shifts]
    nearer = [
        [jnp.where(sources[j] < sources[i], 1.0, 0.0) for j in range(count)] for i in range(count)
    ]
    ambient = 0.5 * jnp.full((SUBLANES, LANES), transfer[7], jnp.float32)
    spread = (1.0 - ambient) / 3.0

    def band(r, carry):
        here = pl.ds(pl.multiple_of(r * SUBLANES, SUBLANES), SUBLANES)
        for x in range(width // LANES):
            at = pl.ds(x * LANES, LANES)
            shade = tinted = log_t = jnp.zeros((SUBLANES, LANES), jnp.float32)
            logs = [part[2, here, at] for part in parts]
            for i, part in enumerate(parts):
                ahead = sum(logs[j] * nearer[i][j] for j in range(count) if j != i)
                passing = jnp.exp2(ahead)
                shade = shade + passing * part[0, here, at]
                tinted = tinted + passing * part[1, here, at]
                log_t = log_t + logs[i]
            half = jnp.tanh(log_t * (-0.5 * LN2))
            opacity = (half + half) / (1.0 + half)
            full = ambient * opacity + spread * shade
            mixed = 0.5 * (full + ambient * tinted)
            for color in range(3):
                out[color, here, at] = transfer[color] * full + transfer[3 + color] * mixed
            out[3, here, at] = opacity
        return carry

    lax.fori_loop(0, rows // SUBLANES, band, 0)


def merge(parts, shifts, transfer):
    _, rows, width = parts[0].shape
    return pl.pallas_call(
        functools.partial(merge_kernel, shifts),
        in_specs=[SMEM] + [VMEM] * len(parts),
        out_specs=VMEM,
        out_shape=jax.ShapeDtypeStruct((4, rows, width), jnp.float32),
        compiler_params=pltpu.CompilerParams(vmem_limit_bytes=16 << 20),
        name="merge",
    )(transfer, *parts)


def on_device(volume, transfer):
    slices, rows, columns = volume.shape
    groups = lax.axis_size("depth")
    total_slices = slices * groups
    width = columns // groups
    slab_a, slab_b, strip_a, strip_b = cut(volume)
    edges = (swap(slab_a, "depth", 0), swap(slab_b, "depth", 1), swap(strip_a, "row", 0), swap(strip_b, "row", 1))
    half = slices // 2
    halves = [(0, half + 1, 0, rows), (half + 1, slices - half - 1, 0, rows)]
    shifts = order_of_shifts(groups)
    parts = []
    counts = (4, len(halves))
    for stage, shift in enumerate(shifts):
        later = shifts[stage + 1] if shift else None
        if stage == 0:
            kernel = functools.partial(inner_kernel, shift, later, halves, total_slices)
            pair = (len(halves), len(halves))
            inner, cells, ahead = call(kernel, transfer, volume, (), (), (), 2, pair, width)
            kernel = functools.partial(rest_kernel, shift, total_slices)
            part, free = call(kernel, transfer, volume, edges, (inner,), (cells,), 0, (4,), width)
        elif shift:
            kernel = functools.partial(full_kernel, shift, later, half, halves, total_slices)
            buffers = (ahead, free)
            part, free, ahead = call(kernel, transfer, volume, edges, (), buffers, 0, counts, width)
        else:
            kernel = functools.partial(full_kernel, shift, None, half, halves, total_slices)
            part, _ = call(kernel, transfer, volume, edges, (), (ahead,), 0, (4,), width, 28)
        if shift:
            pairs = [(i, (i + shift) % groups) for i in range(groups)]
            part = lax.ppermute(part, "depth", pairs)
        parts.append(part)
    return merge(parts, shifts, transfer)


def order_of_shifts(groups):
    return sorted(range(1, groups), key=lambda s: -min(s, groups - s)) + [0]


def solution(mesh):
    in_specs = (P("depth", "row", None), P())
    out_specs = P(None, "row", "depth")

    return jax.shard_map(on_device, mesh=mesh, in_specs=in_specs, out_specs=out_specs, check_vma=False)
```
